32 devices in a mesh: seq: 16 (over z, x, core), kv: 2 (over y).
Axes of the slice: x: 2, y: 2, z: 4, core: 2. Of those that a mesh axis runs over, the one named last changes fastest.
Arguments:
- q_band: bfloat16 [4096, 4096], P('seq', 'kv'), may hold values from -10 to 10
- k_band: bfloat16 [4096, 512], P('seq', 'kv'), may hold values from -10 to 10
- v_band: bfloat16 [4096, 512], P('seq', 'kv'), may hold values from -6 to 6
- sink_band: float32 [64], P('kv'), may hold values from -1 to 3
- q_doc: bfloat16 [4096, 4096], P('seq', 'kv'), may hold values from -10 to 10
- k_doc: bfloat16 [4096, 512], P('seq', 'kv'), may hold values from -10 to 10
- v_doc: bfloat16 [4096, 512], P('seq', 'kv'), may hold values from -6 to 6
- sink_doc: float32 [64], P('kv'), may hold values from -1 to 3
- doc_starts: int32 [16], replicated, may hold values from 0 to 4095, as said below
- source_lists: int32 [16, 8], P('seq'), may hold values from -1 to 14, as said below
Outputs:
- out_band: bfloat16 [4096, 4096], P(('seq', 'kv'))
- out_doc: bfloat16 [4096, 4096], P(('seq', 'kv'))
The draws below stay inside these ranges and needn't reach their ends.
Inputs may be any that keep to these rules, and one draw needn't show every extreme that they name: `doc_starts`: Non-decreasing, the first entry 0; equal neighbours mark empty documents; no document holds more than 2048 tokens and one holds exactly 2048. `source_lists`: row s names, in falling order, every earlier shard from s - 1 down to the shard in which the document holding shard s's first token begins; -1 fills the remaining entries. Some row names 8 shards.
All inputs are finite; a program needn't handle non-finite values.
Results may differ from the reference program's by a relative error of at most 0.0039.
Values may be sent and summed in bfloat16 or wider, within the bound.
No kernel may reach another device: no remote copies, remote signals or barrier semaphores. Data moves between devices by JAX's collectives and lax.ppermute only.
A program may use at most 64 MiB of HBM per device.

```python
import jax
import jax.numpy as jnp
from jax import lax

HD = 64
KV = 8
G = 8
WIN = 128
BACK = 8
TOK_DEV = 256
HQ = 64
TOKENS = 4096
MAXDOC = 2048
NINT = 5
NEXTRA = 8
N_SEQ = 16


def doc_layout(key):
    base_key = jax.random.fold_in(key, 7)
    tail_key, offset_key, extra_key = jax.random.split(base_key, 3)
    tail_len = jax.random.randint(tail_key, (), 1, TOK_DEV, dtype=jnp.int32)
    edge_pos = TOKENS - tail_len - MAXDOC
    half_doc = MAXDOC // 2
    spaced = jnp.arange(NINT, dtype=jnp.int32) * half_doc
    offsets = jax.random.randint(offset_key, (NINT,), 0, half_doc, dtype=jnp.int32)
    cuts = jnp.where(spaced < edge_pos, jnp.minimum(spaced + offsets, edge_pos - 1), 0)
    extra = jax.random.randint(extra_key, (NEXTRA,), 0, edge_pos, dtype=jnp.int32)
    fixed_cuts = jnp.stack([edge_pos, TOKENS - tail_len]).astype(jnp.int32)
    starts = jnp.concatenate([jnp.zeros((1,), jnp.int32), cuts.astype(jnp.int32), extra, fixed_cuts])
    starts = jnp.sort(starts)
    shard_ids = jnp.arange(N_SEQ, dtype=jnp.int32)
    first_tok = shard_ids * TOK_DEV
    doc_begin = jnp.max(jnp.where(starts[None, :] <= first_tok[:, None], starts[None, :], 0), axis=1)
    begin_shard = doc_begin // TOK_DEV
    candidate = shard_ids[:, None] - 1 - jnp.arange(BACK, dtype=jnp.int32)[None, :]
    lists = jnp.where(candidate >= begin_shard[:, None], candidate, -1).astype(jnp.int32)
    return (starts, lists)


def query_draw(key, layer_id):
    noise_key = jax.random.fold_in(key, 100 + layer_id)
    values = 2.0 * jnp.clip(jax.random.normal(noise_key, (TOKENS, KV, G, HD), jnp.float32), -4.0, 4.0)
    return values.reshape(TOKENS, KV * G * HD).astype(jnp.bfloat16)


def key_draw(key, layer_id):
    noise_key = jax.random.fold_in(key, 200 + layer_id)
    values = jnp.clip(jax.random.normal(noise_key, (TOKENS, KV, HD), jnp.float32), -4.0, 4.0)
    return values.reshape(TOKENS, KV * HD).astype(jnp.bfloat16)


def draw_q_band(key, part):
    return query_draw(key, 0)


def draw_k_band(key, part):
    return key_draw(key, 0)


def draw_q_doc(key, part):
    return query_draw(key, 1)


def draw_k_doc(key, part):
    return key_draw(key, 1)


def draw_doc_starts(key, part):
    return doc_layout(key)[0]


def draw_source_lists(key, part):
    return doc_layout(key)[1]


def block_levels(rng, dims, cuts, smallest, high):
    loudness = 1.0
    for position, blocks in cuts:
        heights = jax.random.uniform(jax.random.fold_in(jax.random.fold_in(rng, 6), position), (blocks,), jnp.float32, smallest / len(cuts), high / len(cuts))
        loudness = loudness * jnp.repeat(jnp.exp(heights), dims[position] // blocks).reshape((-1,) + (1,) * (len(dims) - 1 - position))
    return loudness


def noise(stream_key, shape, width, most, cuts=(), kind=jnp.bfloat16):
    entries = jax.random.normal(stream_key, shape, jnp.float32) * width
    if len(cuts) > 0:
        entries = block_levels(stream_key, shape, cuts, -0.22, 0.18) * entries
    return jnp.clip(entries, min=-most, max=most).astype(kind)


def setup_inputs(seed: int = 0) -> dict:
    streams_of = jax.random.split(jax.random.key(seed), 11)
    q_band = draw_q_band(jax.random.fold_in(streams_of[10], 71), 0)
    k_band = draw_k_band(jax.random.fold_in(streams_of[10], 71), 0)
    v_band = noise(streams_of[2], (TOKENS, KV * HD), 1.0, 6.0, ((0, 16), (1, 2)))
    sink_band = jnp.clip(-1.0 + 4.0 * jax.random.uniform(streams_of[3], (HQ,), jnp.float32) ** block_levels(streams_of[3], (HQ,), ((0, 2),), -0.2, 0.2), -1.0, 3.0)
    q_doc = draw_q_doc(jax.random.fold_in(streams_of[10], 71), 0)
    k_doc = draw_k_doc(jax.random.fold_in(streams_of[10], 71), 0)
    v_doc = noise(streams_of[6], (TOKENS, KV * HD), 1.0, 6.0, ((0, 16), (1, 2)))
    sink_doc = jnp.clip(-1.0 + 4.0 * jax.random.uniform(streams_of[7], (HQ,), jnp.float32) ** block_levels(streams_of[7], (HQ,), ((0, 2),), -0.2, 0.2), -1.0, 3.0)
    doc_starts = draw_doc_starts(jax.random.fold_in(streams_of[10], 71), 0)
    source_lists = draw_source_lists(jax.random.fold_in(streams_of[10], 71), 0)
    return dict(q_band=q_band, k_band=k_band, v_band=v_band, sink_band=sink_band, q_doc=q_doc, k_doc=k_doc, v_doc=v_doc, sink_doc=sink_doc, doc_starts=doc_starts, source_lists=source_lists)


def doc_number(doc_starts, positions):
    return jnp.sum((doc_starts[None, :] <= positions[:, None]).astype(jnp.int32), axis=1)


def attend(queries, key_rows, value_rows, sink_logits, allowed):
    scores = jnp.einsum("qgd,kd->gqk", queries.astype(jnp.float32), key_rows.astype(jnp.float32)) * (HD ** -0.5)
    scores = jnp.where(allowed[None, :, :], scores, -jnp.inf)
    top_logit = jnp.maximum(sink_logits[:, None], jnp.max(scores, axis=2))
    exponent = jnp.exp(scores - top_logit[:, :, None])
    totals = jnp.exp(sink_logits[:, None] - top_logit) + jnp.sum(exponent, axis=2)
    weights = lax.optimization_barrier(exponent.astype(jnp.bfloat16)).astype(jnp.float32)
    numerator = jnp.einsum("gqk,kd->gqd", weights, value_rows.astype(jnp.float32))
    return jnp.transpose(numerator / totals[:, :, None], (1, 0, 2)).astype(jnp.bfloat16)


def layer_output(queries, key_rows, value_rows, sinks, doc_starts, source_lists, banded):
    span_rows = WIN if banded else BACK * TOK_DEV
    query_heads = queries.reshape(TOKENS, KV, G, HD)
    key_heads = key_rows.reshape(TOKENS, KV, HD)
    value_heads = value_rows.reshape(TOKENS, KV, HD)
    key_padded = jnp.concatenate([jnp.zeros((span_rows, KV, HD), key_rows.dtype), key_heads], axis=0)
    value_padded = jnp.concatenate([jnp.zeros((span_rows, KV, HD), value_rows.dtype), value_heads], axis=0)
    sink_table = sinks.reshape(KV, G)
    zero_index = jnp.zeros((), jnp.int32)

    def per_block(flat_index):
        shard_index = flat_index // KV
        kv_head = flat_index % KV
        row_start = shard_index * TOK_DEV
        query_block = lax.dynamic_slice(query_heads, (row_start, kv_head, zero_index, zero_index), (TOK_DEV, 1, G, HD))[:, 0]
        key_block = lax.dynamic_slice(key_padded, (row_start, kv_head, zero_index), (span_rows + TOK_DEV, 1, HD))[:, 0]
        value_block = lax.dynamic_slice(value_padded, (row_start, kv_head, zero_index), (span_rows + TOK_DEV, 1, HD))[:, 0]
        query_pos = row_start + jnp.arange(TOK_DEV, dtype=jnp.int32)
        key_pos = row_start - span_rows + jnp.arange(span_rows + TOK_DEV, dtype=jnp.int32)
        same_doc = doc_number(doc_starts, query_pos)[:, None] == doc_number(doc_starts, key_pos)[None, :]
        allowed = same_doc & (key_pos[None, :] <= query_pos[:, None]) & (key_pos[None, :] >= 0)
        if banded:
            allowed = allowed & (query_pos[:, None] - key_pos[None, :] < WIN)
        else:
            key_shard = jnp.floor_divide(key_pos, TOK_DEV)
            row_list = lax.dynamic_index_in_dim(source_lists, shard_index, 0, keepdims=False)
            named = jnp.any((row_list[None, :] == key_shard[:, None]) & (row_list[None, :] >= 0), axis=1)
            listed = (key_shard == shard_index) | named
            allowed = allowed & listed[None, :]
        sink_row = lax.dynamic_index_in_dim(sink_table, kv_head, 0, keepdims=False)
        return attend(query_block, key_block, value_block, sink_row, allowed)

    blocks = lax.map(per_block, jnp.arange(N_SEQ * KV, dtype=jnp.int32))
    blocks = blocks.reshape(N_SEQ, KV, TOK_DEV, G, HD)
    blocks = jnp.transpose(blocks, (0, 2, 1, 3, 4))
    return blocks.reshape(TOKENS, KV * G * HD)


def reference(q_band, k_band, v_band, sink_band, q_doc, k_doc, v_doc, sink_doc, doc_starts, source_lists):
    out_band = layer_output(q_band, k_band, v_band, sink_band, doc_starts, source_lists, True)
    out_doc = layer_output(q_doc, k_doc, v_doc, sink_doc, doc_starts, source_lists, False)
    return (out_band, out_doc)
```

```python
import functools
import jax
import jax.numpy as jnp
from jax import lax
from jax.experimental import pallas as pl
from jax.experimental.pallas import tpu as pltpu
from jax.sharding import PartitionSpec as P

HD = 64
G = 8
WIN = 128
BACK = 8
LOG2E = 1.4426950408889634
SCORE_SCALE = HD ** (-0.5) * LOG2E
NEG = -1e30


def start_of(starts_ref, position):
    found = jnp.int32(0)
    for i in range(starts_ref.shape[0]):
        entry = starts_ref[i]
        found = jnp.where(entry <= position, jnp.maximum(found, entry), found)
    return found


def start_row(starts_ref, positions):
    found = jnp.zeros_like(positions)
    for i in range(starts_ref.shape[0]):
        entry = starts_ref[i]
        found = jnp.where(positions >= entry, jnp.maximum(found, entry), found)
    return found


def fold_in(state, key_block, query_cols, value_rows, kept):
    top, total, acc = state
    scores = jnp.dot(key_block, query_cols, preferred_element_type=jnp.float32)
    if kept is not None:
        scores = jnp.where(kept, scores, NEG)
    new_top = jnp.maximum(top, jnp.max(scores, axis=0, keepdims=True) * SCORE_SCALE)
    weight = jnp.exp2(scores * SCORE_SCALE - new_top)
    fading = jnp.exp2(top - new_top)
    total = total * fading + jnp.sum(weight, axis=0, keepdims=True)
    acc = acc * fading + jnp.dot(
        value_rows, weight.astype(jnp.bfloat16), preferred_element_type=jnp.float32
    )
    return new_top, total, acc


def slot_cols(query_cols, slot, slots):
    if slots == 1:
        return query_cols
    empty = jnp.zeros_like(query_cols)
    return jnp.concatenate([query_cols if i == slot else empty for i in range(slots)], axis=0)


def doc_body(plan, *refs):
    first, last, grp, heads, rows = plan.first, plan.last, plan.grp, plan.heads, plan.rows
    refs = list(refs)
    where_ref, starts_ref, list_ref, sink_ref = refs[:4]
    del refs[:4]
    mate_list_ref = refs.pop(0) if grp == 2 else None
    query_refs = [refs.pop(0) for _ in range(grp)]
    unit_refs = [refs.pop(0) for _ in range(plan.units)]
    if not first:
        acc_in, stat_in = refs.pop(0), refs.pop(0)
    if last:
        piece_refs = [refs.pop(0) for _ in range(2 * grp if plan.pieces else 1)]
    else:
        acc_out, stat_out = refs.pop(0), refs.pop(0)
    value_ref, start_ref, flag_ref, acc_ref, stat_ref = refs
    step = pl.program_id(0)
    pairs = G // 2
    own_shard = where_ref[0]
    shards = [own_shard, own_shard ^ 1][:grp]
    width = heads * HD
    blocks = [(n, r) for n in range(plan.units) for r in range(grp)]
    key_shards = []
    for n, r in blocks:
        key_shards.append(shards[r] - where_ref[4 + n])

    @pl.when(step == 0)
    def _():
        for n in range(plan.units):
            unit = unit_refs[n][...]
            if width % 128 == 0:
                value_ref[n] = unit[:, width:].T
            else:
                value_ref[n] = unit.T[width:]
        for a in range(grp):
            q_low = shards[a] * rows
            start_low = start_of(starts_ref, q_low)
            start_high = start_of(starts_ref, q_low + rows - 1)
            positions = q_low + lax.broadcasted_iota(jnp.int32, (8, rows), 1)
            start_ref[a] = start_row(starts_ref, positions)
            if a == 1:
                mate_row = mate_list_ref[...].astype(jnp.float32)[:1]
                lanes = lax.broadcasted_iota(jnp.int32, mate_row.shape, 1)
            for b, (n, r) in enumerate(blocks):
                shard = key_shards[b]
                if a == 0:
                    named = shard == shards[0]
                    for i in range(BACK):
                        named = named | (list_ref[0, i] == shard)
                else:
                    same = (mate_row == shard.astype(jnp.float32)) & (lanes < BACK)
                    named = (shard == shards[1]) | (jnp.max(same.astype(jnp.float32)) > 0.5)
                k_low = shard * rows
                live = named & (shard >= 0) & (shard <= shards[a]) & (k_low + rows > start_low)
                whole = (k_low >= start_high) & (shard < shards[a])
                flag_ref[a, b] = jnp.where(live, jnp.where(whole, 2, 1), 0)

    head = step // pairs
    for a in range(grp):
        span = slice(a * rows, (a + 1) * rows)
        if first:
            for e in range(2):
                sink = sink_ref[where_ref[1] * heads * G + 2 * step + e] * LOG2E
                stat_ref[e : e + 1, span] = jnp.full((1, rows), sink, jnp.float32)
            stat_ref[2:4, span] = jnp.ones((2, rows), jnp.float32)
            acc_ref[:, span] = jnp.zeros((2 * HD, rows), jnp.float32)
    if not first:
        acc_ref[...] = acc_in[0]
        stat_ref[...] = stat_in[0]

    value_span = pl.ds(pl.multiple_of(head * HD, HD), HD)
    for a in range(grp):
        span = slice(a * rows, (a + 1) * rows)
        turned = query_refs[a][...].T
        cols = []
        for e in range(2):
            col = turned[e * HD : (e + 1) * HD]
            if heads > 1:
                empty = jnp.zeros_like(col)
                col = jnp.concatenate(
                    [jnp.where(head == i, col, empty) for i in range(heads)], axis=0
                )
            cols.append(col)
        for b, (n, r) in enumerate(blocks):
            key_block = unit_refs[n].at[r * rows : (r + 1) * rows, :width]
            value_rows = value_ref.at[n, value_span, r * rows : (r + 1) * rows]

            def work(masked, a=a, b=b, span=span, key_block=key_block, value_rows=value_rows):
                kept = None
                if masked:
                    u = key_shards[b] * rows + lax.broadcasted_iota(jnp.int32, (rows, rows), 0)
                    t = shards[a] * rows + lax.broadcasted_iota(jnp.int32, (rows, rows), 1)
                    kept = (u <= t) & (u >= start_ref[a][:1])
                for e in range(2):
                    state = (
                        stat_ref[e : e + 1, span],
                        stat_ref[2 + e : 3 + e, span],
                        acc_ref[e * HD : (e + 1) * HD, span],
                    )
                    top, total, acc = fold_in(state, key_block[...], cols[e], value_rows[...], kept)
                    stat_ref[e : e + 1, span] = top
                    stat_ref[2 + e : 3 + e, span] = total
                    acc_ref[e * HD : (e + 1) * HD, span] = acc

            pl.when(flag_ref[a, b] == 1)(functools.partial(work, True))
            pl.when(flag_ref[a, b] == 2)(functools.partial(work, False))

    if not last:
        acc_out[0] = acc_ref[...]
        stat_out[0] = stat_ref[...]
        return
    for a in range(grp):
        span = slice(a * rows, (a + 1) * rows)
        parts = [
            acc_ref[e * HD : (e + 1) * HD, span] / stat_ref[2 + e : 3 + e, span] for e in range(2)
        ]
        result = jnp.concatenate(parts, axis=0).T.astype(jnp.bfloat16)
        if not plan.pieces:
            piece_refs[0][...] = result
            continue
        half = rows // 2
        side = where_ref[2]
        low, high = result[:half], result[half:]
        piece_refs[2 * a][...] = jnp.where(side == 0, low, high)
        piece_refs[2 * a + 1][...] = jnp.where(side == 0, high, low)


class DocPlan:
    def __init__(self, first, last, grp, heads, units, rows, pieces):
        self.first, self.last, self.grp, self.heads = first, last, grp, heads
        self.units, self.rows, self.pieces = units, rows, pieces


def doc_call(plan, where, starts, sources, sinks, mate_rows, queries, units, state, columns):
    grp, heads, rows = plan.grp, plan.heads, plan.rows
    steps = heads * G // 2
    width = heads * HD
    smem = pl.BlockSpec(memory_space=pltpu.SMEM)
    args = [where, starts, sources, sinks]
    specs = [smem, smem, smem]
    if grp == 2:
        args.append(mate_rows)
        specs.append(pl.BlockSpec((16, 128), lambda j, w: (rows // 16, 0)))
    args += list(queries)
    specs.append(pl.BlockSpec((rows, 128), lambda j, w: (0, w[1] * steps + j)))
    if grp == 2:
        specs.append(pl.BlockSpec((rows, 128), lambda j, w: (0, j)))
    for unit in units:
        args.append(unit)
        specs.append(pl.BlockSpec((grp * rows, 2 * width), lambda j, w: (0, 0)))
    lanes = grp * rows
    state_specs = [
        pl.BlockSpec((1, 2 * HD, lanes), lambda j, w: (j, 0, 0)),
        pl.BlockSpec((1, 8, lanes), lambda j, w: (j, 0, 0)),
    ]
    state_shapes = [
        jax.ShapeDtypeStruct((steps, 2 * HD, lanes), jnp.float32),
        jax.ShapeDtypeStruct((steps, 8, lanes), jnp.float32),
    ]
    aliases = {}
    if not plan.first:
        if not plan.last:
            aliases = {len(args): 0, len(args) + 1: 1}
        args += list(state)
        specs += state_specs
    if not plan.last:
        out_shape, out_specs = state_shapes, state_specs
    elif plan.pieces:
        half = rows // 2
        out_shape = [jax.ShapeDtypeStruct((half, columns), jnp.bfloat16)]
        out_specs = [pl.BlockSpec((half, 128), lambda j, w: (0, w[3] * steps + j))]
        for _ in range(2 * grp - 1):
            out_shape.append(jax.ShapeDtypeStruct((half, steps * 128), jnp.bfloat16))
            out_specs.append(pl.BlockSpec((half, 128), lambda j, w: (0, j)))
    else:
        out_shape = [jax.ShapeDtypeStruct((rows, steps * 128), jnp.bfloat16)]
        out_specs = [pl.BlockSpec((rows, 128), lambda j, w: (0, j))]
    blocks = grp * plan.units
    return pl.pallas_call(
        functools.partial(doc_body, plan),
        out_shape=out_shape,
        grid_spec=pltpu.PrefetchScalarGridSpec(
            num_scalar_prefetch=1,
            grid=(steps,),
            in_specs=specs,
            out_specs=out_specs,
            scratch_shapes=[
                pltpu.VMEM((plan.units, width, grp * rows), jnp.bfloat16),
                pltpu.VMEM((grp, 8, rows), jnp.int32),
                pltpu.SMEM((grp, blocks), jnp.int32),
                pltpu.VMEM((2 * HD, lanes), jnp.float32),
                pltpu.VMEM((8, lanes), jnp.float32),
            ],
        ),
        input_output_aliases=aliases,
        compiler_params=pltpu.CompilerParams(
            dimension_semantics=("arbitrary",), vmem_limit_bytes=48 * 1024 * 1024
        ),
        name="doc_attention",
    )(*args)


def band_body(heads, rows, pieces, where_ref, starts_ref, sink_ref, query_ref, key_ref, value_ref, rim_ref, *refs):
    out_refs, (keys, values, start_ref) = refs[:-3], refs[-3:]
    step = pl.program_id(0)
    width = heads * HD
    low = where_ref[0] * rows

    @pl.when(step == 0)
    def _():
        rim = rim_ref[...]
        keys[:WIN] = rim[:, :width]
        keys[WIN:] = key_ref[...]
        if width % 128 == 0:
            values[:, :WIN] = rim[:, width:].T
        else:
            values[:, :WIN] = rim.T[width:]
        values[:, WIN:] = value_ref[...].T
        positions = low + lax.broadcasted_iota(jnp.int32, (8, rows), 1)
        start_ref[...] = start_row(starts_ref, positions)

    head = step // (G // 2)
    turned = query_ref[...].T
    value_span = pl.ds(pl.multiple_of(head * HD, HD), HD)
    finished = []
    for tile in range(rows // WIN):
        span = slice(tile * WIN, (tile + 1) * WIN)
        u = low + (tile - 1) * WIN + lax.broadcasted_iota(jnp.int32, (2 * WIN, WIN), 0)
        t = low + tile * WIN + lax.broadcasted_iota(jnp.int32, (2 * WIN, WIN), 1)
        kept = (u <= t) & (u > t - WIN) & (u >= start_ref[:1, span])
        parts = []
        for e in range(2):
            col = turned[e * HD : (e + 1) * HD, span]
            if heads > 1:
                empty = jnp.zeros_like(col)
                col = jnp.concatenate(
                    [jnp.where(head == i, col, empty) for i in range(heads)], axis=0
                )
            sink = sink_ref[2 * step + e] * LOG2E
            state = (
                jnp.full((1, WIN), sink, jnp.float32),
                jnp.ones((1, WIN), jnp.float32),
                jnp.zeros((HD, WIN), jnp.float32),
            )
            key_span = slice(tile * WIN, (tile + 2) * WIN)
            top, total, acc = fold_in(state, keys[key_span], col, values[value_span, key_span], kept)
            parts.append(acc / total)
        finished.append(jnp.concatenate(parts, axis=0).T.astype(jnp.bfloat16))
    if pieces:
        side = where_ref[2]
        out_refs[0][...] = jnp.where(side == 0, finished[0], finished[1])
        out_refs[1][...] = jnp.where(side == 0, finished[1], finished[0])
    else:
        for tile, value in enumerate(finished):
            out_refs[0][tile * WIN : (tile + 1) * WIN] = value


def band_call(where, starts, sinks, queries, keys, value_rows, rim, heads, rows, pieces, columns):
    steps = heads * G // 2
    width = heads * HD
    smem = pl.BlockSpec(memory_space=pltpu.SMEM)
    if pieces:
        out_shape = [
            jax.ShapeDtypeStruct((WIN, columns), jnp.bfloat16),
            jax.ShapeDtypeStruct((WIN, steps * 128), jnp.bfloat16),
        ]
        out_specs = [
            pl.BlockSpec((WIN, 128), lambda j, w: (0, w[2] * steps + j)),
            pl.BlockSpec((WIN, 128), lambda j, w: (0, j)),
        ]
    else:
        out_shape = [jax.ShapeDtypeStruct((rows, steps * 128), jnp.bfloat16)]
        out_specs = [pl.BlockSpec((rows, 128), lambda j, w: (0, j))]
    fixed = lambda j, w: (0, 0)
    return pl.pallas_call(
        functools.partial(band_body, heads, rows, pieces),
        out_shape=out_shape,
        grid_spec=pltpu.PrefetchScalarGridSpec(
            num_scalar_prefetch=1,
            grid=(steps,),
            in_specs=[
                smem,
                smem,
                pl.BlockSpec((rows, 128), lambda j, w: (0, j)),
                pl.BlockSpec((rows, width), fixed),
                pl.BlockSpec((rows, width), fixed),
                pl.BlockSpec((WIN, 2 * width), fixed),
            ],
            out_specs=out_specs,
            scratch_shapes=[
                pltpu.VMEM((rows + WIN, width), jnp.bfloat16),
                pltpu.VMEM((width, rows + WIN), jnp.bfloat16),
                pltpu.VMEM((8, rows), jnp.int32),
            ],
        ),
        compiler_params=pltpu.CompilerParams(
            dimension_semantics=("arbitrary",), vmem_limit_bytes=48 * 1024 * 1024
        ),
        name="band_attention",
    )(where, starts, sinks, queries, keys, value_rows, rim)


def shifted(value, steps):
    count = lax.axis_size("seq")
    return lax.ppermute(value, "seq", [(i, i + steps) for i in range(count - steps)])


def swapped(value, bit):
    count = lax.axis_size("seq")
    return lax.ppermute(value, "seq", [(i, i ^ bit) for i in range(count)])


def relay(result):
    return lax.all_to_all(result, "kv", split_axis=0, concat_axis=1, tiled=True)


def paired_program(
    q_band, k_band, v_band, sink_band, q_doc, k_doc, v_doc, sink_doc, doc_starts, source_lists
):
    rows = q_band.shape[0]
    heads = k_band.shape[1] // HD
    mine = heads // 2
    width = mine * HD
    columns = 2 * q_band.shape[1]
    shard, side = lax.axis_index("seq"), lax.axis_index("kv")
    core = shard % 2
    layer = shard // 2 % 2
    flip = 4 * layer - 2

    def place(*dists):
        return jnp.stack([shard, core, side, 2 * side + core, *dists]).astype(jnp.int32)

    listed = jnp.zeros((16, 2 * width), jnp.bfloat16)
    listed = lax.dynamic_update_slice(listed, source_lists.astype(jnp.bfloat16), (0, 0))

    def half(value, which, size):
        return lax.dynamic_slice_in_dim(value, which * size, size, axis=1)

    away = jnp.concatenate([half(k_doc, 1 - core, width), half(v_doc, 1 - core, width)], axis=1)
    away = jnp.concatenate([away, listed], axis=0)
    near = swapped(away, 1)
    kept = jnp.concatenate([half(k_doc, core, width), half(v_doc, core, width)], axis=1)
    unit = jnp.concatenate([kept, near[:rows]], axis=0)
    rim = jnp.concatenate([k_band[rows - WIN :], v_band[rows - WIN :]], axis=1)
    rim = shifted(rim, 1)
    q_mate = swapped(half(q_doc, 1 - core, mine * G * HD), 1)
    back4 = shifted(unit, 4)
    back8 = shifted(unit, 8)
    cross0 = swapped(unit, 2)
    cross4 = swapped(back4, 2)
    cross8 = swapped(back8, 2)
    band_out, band_send = band_call(
        place(), doc_starts, sink_band, q_band, k_band, v_band, rim, heads, rows, True, columns
    )
    band_got = lax.ppermute(band_send, "kv", [(0, 1), (1, 0)])
    out_band = lax.dynamic_update_slice(band_out, band_got, (0, (1 - side) * q_band.shape[1]))

    def doc(first, last, units, dists, state):
        plan = DocPlan(first, last, 2, mine, len(units), rows, True)
        return doc_call(
            plan, place(*dists), doc_starts, source_lists, sink_doc, near, (q_doc, q_mate), units, state, columns
        )

    state = doc(True, False, (unit, cross0), (0, flip), None)
    state = doc(False, False, (back4, cross4), (4, 4 + flip), state)
    out_doc, *sends = doc(False, True, (back8, cross8), (8, 8 + flip), state)
    size = mine * G * HD
    for mask, send in zip((1, 2, 3), sends):
        count = 2 * lax.axis_size("seq")
        got = lax.ppermute(send, ("seq", "kv"), [(i, i ^ mask) for i in range(count)])
        source = ((2 * side + core) ^ (mask & 1) * 2 ^ (mask >> 1)) * size
        out_doc = lax.dynamic_update_slice(out_doc, got, (0, source))
    return out_band, out_doc


def plain_program(
    q_band, k_band, v_band, sink_band, q_doc, k_doc, v_doc, sink_doc, doc_starts, source_lists
):
    rows = q_band.shape[0]
    heads = k_band.shape[1] // HD
    shard = lax.axis_index("seq")

    def place(*dists):
        return jnp.stack([shard, 0, 0, 0, *dists]).astype(jnp.int32)

    rim = jnp.concatenate([k_band[rows - WIN :], v_band[rows - WIN :]], axis=1)
    rim = shifted(rim, 1)
    unit = jnp.concatenate([k_doc, v_doc], axis=1)
    units = [unit] + [shifted(unit, d) for d in range(1, BACK + 1)]
    band = band_call(
        place(), doc_starts, sink_band, q_band, k_band, v_band, rim, heads, rows, False, None
    )[0]
    plan = DocPlan(True, True, 1, heads, BACK + 1, rows, False)
    doc = doc_call(
        plan, place(*range(BACK + 1)), doc_starts, source_lists, sink_doc, None,
        (q_doc,), units, None, None,
    )[0]
    return relay(band), relay(doc)


def solution(mesh):
    placed = (
        P("seq", "kv"),
        P("seq", "kv"),
        P("seq", "kv"),
        P("kv"),
        P("seq", "kv"),
        P("seq", "kv"),
        P("seq", "kv"),
        P("kv"),
        P(),
        P("seq", None),
    )

    def per_device(*args):
        heads = args[1].shape[1] // HD
        even = heads % 4 == 0 and mesh.shape["kv"] == 2 and mesh.shape["seq"] % 4 == 0
        return (paired_program if even else plain_program)(*args)

    return jax.shard_map(
        per_device,
        mesh=mesh,
        in_specs=placed,
        out_specs=(P(("seq", "kv"), None), P(("seq", "kv"), None)),
        check_vma=False,
    )
```

```python
import functools
import jax
import jax.numpy as jnp
from jax import lax
from jax.experimental import pallas as pl
from jax.experimental.pallas import tpu as pltpu
from jax.sharding import PartitionSpec as P

HD = 64
G = 8
WIN = 128
BACK = 8
LOG2E = 1.4426950408889634
SCORE_SCALE = HD ** (-0.5) * LOG2E
NEG = -1e30
SAFE_TOTAL = 2.0**100
NEVER = 2**30
PARAMS = pltpu.CompilerParams(
    dimension_semantics=("arbitrary",), vmem_limit_bytes=48 * 1024 * 1024
)


def start_of(starts_ref, position):
    found = jnp.int32(0)
    for i in range(starts_ref.shape[0]):
        entry = starts_ref[i]
        found = jnp.where(entry <= position, jnp.maximum(found, entry), found)
    return found


def start_row(starts_ref, positions):
    found = jnp.zeros_like(positions)
    for i in range(starts_ref.shape[0]):
        entry = starts_ref[i]
        found = jnp.where(positions >= entry, jnp.maximum(found, entry), found)
    return found


def score(key_block, query_cols):
    return jnp.dot(key_block, query_cols, preferred_element_type=jnp.float32) * SCORE_SCALE


def plain_weights(key_block, query_cols, kept):
    weight = jnp.where(kept, jnp.exp2(score(key_block, query_cols)), 0.0)
    return weight.astype(jnp.bfloat16), jnp.sum(weight, axis=0, keepdims=True)


def weigh(value_rows, weight):
    return jnp.dot(value_rows, weight, preferred_element_type=jnp.float32)


def topped(state, key_block, query_cols, value_rows, kept):
    top, total, acc = state
    scores = jnp.where(kept, score(key_block, query_cols), NEG)
    new_top = jnp.maximum(top, jnp.max(scores, axis=0, keepdims=True))
    weight = jnp.exp2(scores - new_top)
    fading = jnp.exp2(top - new_top)
    total = total * fading + jnp.sum(weight, axis=0, keepdims=True)
    acc = acc * fading + weigh(value_rows, weight.astype(jnp.bfloat16))
    return new_top, total, acc


def slotted(col, head, heads):
    if heads == 1:
        return col
    empty = jnp.zeros_like(col)
    return jnp.concatenate([jnp.where(head == i, col, empty) for i in range(heads)], axis=0)


def overflowed(total):
    return jnp.logical_not(jnp.max(total) <= SAFE_TOTAL)


def sink_lanes(sink_ref, first, count, rows):
    return jnp.concatenate(
        [jnp.full((1, rows), sink_ref[first + e] * LOG2E, jnp.float32) for e in range(count)], axis=1
    )


class DocPlan:
    def __init__(self, first, last, grp, heads, earlier, units, rows, pieces):
        self.first, self.last, self.grp, self.heads = first, last, grp, heads
        self.earlier, self.units, self.rows, self.pieces = earlier, units, rows, pieces


def doc_body(plan, *refs):
    first, last, grp, heads, rows = plan.first, plan.last, plan.grp, plan.heads, plan.rows
    count = plan.earlier + plan.units
    refs = list(refs)
    where_ref, starts_ref, list_ref, sink_ref = refs[:4]
    del refs[:4]
    mate_list_ref = refs.pop(0) if grp == 2 else None
    query_refs = [refs.pop(0) for _ in range(grp)]
    unit_refs = [refs.pop(0) for _ in range(count)]
    if not first:
        acc_in, total_in = refs.pop(0), refs.pop(0)
    if last:
        piece_refs = [refs.pop(0) for _ in range(2 * grp if plan.pieces else 1)]
    else:
        acc_out, total_out = refs.pop(0), refs.pop(0)
    value_ref, bound_ref, flag_ref, acc_ref, total_ref = refs
    step = pl.program_id(0)
    own_shard = where_ref[0]
    shards = [own_shard, own_shard ^ 1][:grp]
    width = heads * HD
    lanes = 2 * grp * rows
    new = range(plan.earlier, count)

    def key_shard(n, r):
        return shards[r] - where_ref[4 + n]

    @pl.when(step == 0)
    def _():
        for n in range(count):
            unit = unit_refs[n][...]
            value_ref[n] = unit[:, width:].T if width % 128 == 0 else unit.T[width:]
        for n in range(count):
            flag_ref[n] = 0
        for a in range(grp):
            q_low = shards[a] * rows
            start_low = start_of(starts_ref, q_low)
            positions = q_low + lax.broadcasted_iota(jnp.int32, (1, rows), 1)
            starts = start_row(starts_ref, positions)
            if a == 1:
                mate_row = mate_list_ref[...].astype(jnp.float32)[:1]
                listed = lax.broadcasted_iota(jnp.int32, mate_row.shape, 1) < BACK
            for n in range(count):
                for r in range(grp):
                    shard = key_shard(n, r)
                    named = shard == shards[a]
                    if a == 0:
                        for i in range(BACK):
                            named = named | (list_ref[0, i] == shard)
                    else:
                        same = (mate_row == shard.astype(jnp.float32)) & listed
                        named = named | (jnp.max(same.astype(jnp.float32)) > 0.5)
                    named = named & (shard >= 0) & (shard <= shards[a])
                    live = named & ((shard + 1) * rows > start_low)
                    flag_ref[n] = flag_ref[n] | live.astype(jnp.int32)
                    bound = jnp.where(named, starts, NEVER)
                    spot = slice(2 * a * rows, 2 * (a + 1) * rows)
                    bound_ref[n, r : r + 1, spot] = jnp.concatenate([bound, bound], axis=1)

    head = step // (G // 2)
    sinks = sink_lanes(sink_ref, where_ref[1] * heads * G + 2 * step, 2, rows)
    sinks = jnp.concatenate([sinks] * grp, axis=1)
    if first:
        total_ref[...] = jnp.exp2(sinks)
        acc_ref[...] = jnp.zeros((HD, lanes), jnp.float32)
    else:
        total_ref[...] = total_in[0]
        acc_ref[...] = acc_in[0]
    cols = []
    for a in range(grp):
        turned = query_refs[a][...].T
        cols += [slotted(turned[e * HD : (e + 1) * HD], head, heads) for e in range(2)]
    cols = jnp.concatenate(cols, axis=1)
    value_span = pl.ds(pl.multiple_of(head * HD, HD), HD)

    def keep(n, r):
        u = key_shard(n, r) * rows + lax.broadcasted_iota(jnp.int32, (rows, lanes), 0)
        kept = u >= bound_ref[n, r : r + 1]
        if n == 0:
            lane = lax.broadcasted_iota(jnp.int32, (1, lanes), 1)
            t = jnp.bitwise_and(lane, rows - 1) + own_shard * rows
            if grp == 2:
                t = jnp.where(lane < 2 * rows, t, t + ((own_shard ^ 1) - own_shard) * rows)
            kept = kept & (u <= t)
        return kept

    def keys_of(n, r):
        return unit_refs[n][r * rows : (r + 1) * rows, :width]

    def values_of(n, r=None):
        span = slice(None) if r is None else slice(r * rows, (r + 1) * rows)
        return value_ref[n, value_span, span]

    def work(n):
        total = total_ref[...]
        weights = []
        for r in range(grp):
            weight, part = plain_weights(keys_of(n, r), cols, keep(n, r))
            weights.append(weight)
            total = total + part
        total_ref[...] = total
        acc_ref[...] += weigh(values_of(n), jnp.concatenate(weights, axis=0))

    for n in new:
        pl.when(flag_ref[n] > 0)(functools.partial(work, n))

    if not last:
        acc_out[0] = acc_ref[...]
        total_out[0] = total_ref[...]
        return

    @pl.when(overflowed(total_ref[...]))
    def _():
        state = sinks, jnp.ones((1, lanes), jnp.float32), jnp.zeros((HD, lanes), jnp.float32)
        for n in range(count):
            for r in range(grp):
                state = topped(state, keys_of(n, r), cols, values_of(n, r), keep(n, r))
        total_ref[...] = state[1]
        acc_ref[...] = state[2]

    result = acc_ref[...] / total_ref[...]
    for a in range(grp):
        parts = [result[:, (2 * a + e) * rows : (2 * a + e + 1) * rows] for e in range(2)]
        block = jnp.concatenate(parts, axis=0).T.astype(jnp.bfloat16)
        if not plan.pieces:
            piece_refs[0][...] = block
            continue
        half = rows // 2
        side = where_ref[2]
        low, high = block[:half], block[half:]
        piece_refs[2 * a][...] = jnp.where(side == 0, low, high)
        piece_refs[2 * a + 1][...] = jnp.where(side == 0, high, low)


def doc_call(plan, where, starts, sources, sinks, mate_rows, queries, units, state, columns):
    grp, heads, rows = plan.grp, plan.heads, plan.rows
    steps = heads * G // 2
    width = heads * HD
    count = plan.earlier + plan.units
    smem = pl.BlockSpec(memory_space=pltpu.SMEM)
    args = [where, starts, sources, sinks]
    specs = [smem, smem, smem]
    if grp == 2:
        args.append(mate_rows)
        specs.append(pl.BlockSpec((16, 128), lambda j, w: (rows // 16, 0)))
    args += list(queries)
    specs.append(pl.BlockSpec((rows, 128), lambda j, w: (0, w[1] * steps + j)))
    if grp == 2:
        specs.append(pl.BlockSpec((rows, 128), lambda j, w: (0, j)))
    for unit in units:
        args.append(unit)
        specs.append(pl.BlockSpec((grp * rows, 2 * width), lambda j, w: (0, 0)))
    lanes = 2 * grp * rows
    state_specs = [
        pl.BlockSpec((1, HD, lanes), lambda j, w: (j, 0, 0)),
        pl.BlockSpec((1, 1, lanes), lambda j, w: (j, 0, 0)),
    ]
    state_shapes = [
        jax.ShapeDtypeStruct((steps, HD, lanes), jnp.float32),
        jax.ShapeDtypeStruct((steps, 1, lanes), jnp.float32),
    ]
    aliases = {}
    if not plan.first:
        if not plan.last:
            aliases = {len(args): 0, len(args) + 1: 1}
        args += list(state)
        specs += state_specs
    if not plan.last:
        out_shape, out_specs = state_shapes, state_specs
    elif plan.pieces:
        half = rows // 2
        out_shape = [jax.ShapeDtypeStruct((half, columns), jnp.bfloat16)]
        out_specs = [pl.BlockSpec((half, 128), lambda j, w: (0, w[3] * steps + j))]
        for _ in range(2 * grp - 1):
            out_shape.append(jax.ShapeDtypeStruct((half, steps * 128), jnp.bfloat16))
            out_specs.append(pl.BlockSpec((half, 128), lambda j, w: (0, j)))
    else:
        out_shape = [jax.ShapeDtypeStruct((rows, steps * 128), jnp.bfloat16)]
        out_specs = [pl.BlockSpec((rows, 128), lambda j, w: (0, j))]
    return pl.pallas_call(
        functools.partial(doc_body, plan),
        out_shape=out_shape,
        grid_spec=pltpu.PrefetchScalarGridSpec(
            num_scalar_prefetch=1,
            grid=(steps,),
            in_specs=specs,
            out_specs=out_specs,
            scratch_shapes=[
                pltpu.VMEM((count, width, grp * rows), jnp.bfloat16),
                pltpu.VMEM((count, grp, lanes), jnp.int32),
                pltpu.SMEM((count,), jnp.int32),
                pltpu.VMEM((HD, lanes), jnp.float32),
                pltpu.VMEM((1, lanes), jnp.float32),
            ],
        ),
        input_output_aliases=aliases,
        compiler_params=PARAMS,
        name="doc_attention",
    )(*args)


def band_body(heads, rows, wide, pieces, where_ref, starts_ref, sink_ref, query_ref, key_ref, value_ref, rim_ref, *refs):
    out_refs, (keys, values, bound_ref, acc_ref, total_ref) = refs[:-5], refs[-5:]
    step = pl.program_id(0)
    width = heads * HD
    low = where_ref[0] * rows
    tiles = rows // WIN
    lanes = wide * WIN

    @pl.when(step == 0)
    def _():
        rim = rim_ref[...]
        keys[:WIN] = rim[:, :width]
        keys[WIN:] = key_ref[...]
        values[:, :WIN] = rim[:, width:].T if width % 128 == 0 else rim.T[width:]
        values[:, WIN:] = value_ref[...].T
        t = low + lax.broadcasted_iota(jnp.int32, (1, rows), 1)
        bound = jnp.maximum(start_row(starts_ref, t), t - (WIN - 1))
        for tile in range(tiles):
            part = bound[:, tile * WIN : (tile + 1) * WIN]
            bound_ref[tile : tile + 1] = jnp.concatenate([part] * wide, axis=1)

    head = step // (G // wide)
    turned = query_ref[...].T
    value_span = pl.ds(pl.multiple_of(head * HD, HD), HD)
    sinks = sink_lanes(sink_ref, wide * step, wide, WIN)

    def cols_of(tile):
        span = slice(tile * WIN, (tile + 1) * WIN)
        cols = [slotted(turned[e * HD : (e + 1) * HD, span], head, heads) for e in range(wide)]
        return jnp.concatenate(cols, axis=1)

    def keep(tile):
        u = lax.broadcasted_iota(jnp.int32, (2 * WIN, lanes), 0) + (low + (tile - 1) * WIN)
        lane = lax.broadcasted_iota(jnp.int32, (1, lanes), 1)
        t = jnp.bitwise_and(lane, WIN - 1) + (low + tile * WIN)
        return (u <= t) & (u >= bound_ref[tile : tile + 1])

    for tile in range(tiles):
        span = slice(tile * WIN, (tile + 2) * WIN)
        weight, part = plain_weights(keys[span], cols_of(tile), keep(tile))
        total_ref[tile : tile + 1] = jnp.exp2(sinks) + part
        acc_ref[tile] = weigh(values[value_span, span], weight)

    @pl.when(overflowed(total_ref[...]))
    def _():
        for tile in range(tiles):
            span = slice(tile * WIN, (tile + 2) * WIN)
            state = sinks, jnp.ones((1, lanes), jnp.float32), jnp.zeros((HD, lanes), jnp.float32)
            state = topped(state, keys[span], cols_of(tile), values[value_span, span], keep(tile))
            total_ref[tile : tile + 1] = state[1]
            acc_ref[tile] = state[2]

    finished = []
    for tile in range(tiles):
        result = acc_ref[tile] / total_ref[tile : tile + 1]
        parts = [result[:, e * WIN : (e + 1) * WIN] for e in range(wide)]
        finished.append(jnp.concatenate(parts, axis=0).T.astype(jnp.bfloat16))
    if pieces:
        side = where_ref[2]
        out_refs[0][...] = jnp.where(side == 0, finished[0], finished[1])
        out_refs[1][...] = jnp.where(side == 0, finished[1], finished[0])
    else:
        for tile, value in enumerate(finished):
            out_refs[0][tile * WIN : (tile + 1) * WIN] = value


def band_call(where, starts, sinks, queries, keys, value_rows, rim, heads, rows, pieces, columns):
    wide = 4
    steps = heads * G // wide
    size = wide * HD
    width = heads * HD
    tiles = rows // WIN
    smem = pl.BlockSpec(memory_space=pltpu.SMEM)
    if pieces:
        out_shape = [
            jax.ShapeDtypeStruct((WIN, columns), jnp.bfloat16),
            jax.ShapeDtypeStruct((WIN, steps * size), jnp.bfloat16),
        ]
        out_specs = [
            pl.BlockSpec((WIN, size), lambda j, w: (0, w[2] * steps + j)),
            pl.BlockSpec((WIN, size), lambda j, w: (0, j)),
        ]
    else:
        out_shape = [jax.ShapeDtypeStruct((rows, steps * size), jnp.bfloat16)]
        out_specs = [pl.BlockSpec((rows, size), lambda j, w: (0, j))]

    def fixed(j, w):
        return (0, 0)

    return pl.pallas_call(
        functools.partial(band_body, heads, rows, wide, pieces),
        out_shape=out_shape,
        grid_spec=pltpu.PrefetchScalarGridSpec(
            num_scalar_prefetch=1,
            grid=(steps,),
            in_specs=[
                smem,
                smem,
                pl.BlockSpec((rows, size), lambda j, w: (0, j)),
                pl.BlockSpec((rows, width), fixed),
                pl.BlockSpec((rows, width), fixed),
                pl.BlockSpec((WIN, 2 * width), fixed),
            ],
            out_specs=out_specs,
            scratch_shapes=[
                pltpu.VMEM((rows + WIN, width), jnp.bfloat16),
                pltpu.VMEM((width, rows + WIN), jnp.bfloat16),
                pltpu.VMEM((tiles, wide * WIN), jnp.int32),
                pltpu.VMEM((tiles, HD, wide * WIN), jnp.float32),
                pltpu.VMEM((tiles, wide * WIN), jnp.float32),
            ],
        ),
        compiler_params=PARAMS,
        name="band_attention",
    )(where, starts, sinks, queries, keys, value_rows, rim)


def shifted(value, steps):
    count = lax.axis_size("seq")
    return lax.ppermute(value, "seq", [(i, i + steps) for i in range(count - steps)])


def swapped(value, bit):
    count = lax.axis_size("seq")
    return lax.ppermute(value, "seq", [(i, i ^ bit) for i in range(count)])


def relay(result):
    return lax.all_to_all(result, "kv", split_axis=0, concat_axis=1, tiled=True)


def paired_program(
    q_band, k_band, v_band, sink_band, q_doc, k_doc, v_doc, sink_doc, doc_starts, source_lists
):
    rows = q_band.shape[0]
    heads = k_band.shape[1] // HD
    mine = heads // 2
    width = mine * HD
    columns = 2 * q_band.shape[1]
    shard, side = lax.axis_index("seq"), lax.axis_index("kv")
    core = shard % 2
    layer = shard // 2 % 2
    flip = 4 * layer - 2

    def place(*dists):
        return jnp.stack([shard, core, side, 2 * side + core, *dists]).astype(jnp.int32)

    listed = jnp.zeros((16, 2 * width), jnp.bfloat16)
    listed = lax.dynamic_update_slice(listed, source_lists.astype(jnp.bfloat16), (0, 0))

    def half(value, which, size):
        return lax.dynamic_slice_in_dim(value, which * size, size, axis=1)

    away = jnp.concatenate([half(k_doc, 1 - core, width), half(v_doc, 1 - core, width)], axis=1)
    away = jnp.concatenate([away, listed], axis=0)
    near = swapped(away, 1)
    kept = jnp.concatenate([half(k_doc, core, width), half(v_doc, core, width)], axis=1)
    unit = jnp.concatenate([kept, near[:rows]], axis=0)
    rim = jnp.concatenate([k_band[rows - WIN :], v_band[rows - WIN :]], axis=1)
    rim = shifted(rim, 1)
    q_mate = swapped(half(q_doc, 1 - core, mine * G * HD), 1)
    back4 = shifted(unit, 4)
    back8 = shifted(unit, 8)
    cross0 = swapped(unit, 2)
    cross4 = swapped(back4, 2)
    cross8 = swapped(back8, 2)
    band_out, band_send = band_call(
        place(), doc_starts, sink_band, q_band, k_band, v_band, rim, heads, rows, True, columns
    )
    band_got = lax.ppermute(band_send, "kv", [(0, 1), (1, 0)])
    out_band = lax.dynamic_update_slice(band_out, band_got, (0, (1 - side) * q_band.shape[1]))

    def doc(first, last, units, dists, earlier, state):
        plan = DocPlan(first, last, 2, mine, earlier, len(units) - earlier, rows, True)
        return doc_call(
            plan, place(*dists), doc_starts, source_lists, sink_doc, near, (q_doc, q_mate), units, state, columns
        )

    units = [unit, cross0, back4, cross4, back8, cross8]
    dists = [0, flip, 4, 4 + flip, 8, 8 + flip]
    state = doc(True, False, units[:3], dists[:3], 0, None)
    state = doc(False, False, units[3:5], dists[3:5], 0, state)
    out_doc, *sends = doc(False, True, units, dists, 5, state)
    size = mine * G * HD
    for mask, send in zip((1, 2, 3), sends):
        count = 2 * lax.axis_size("seq")
        got = lax.ppermute(send, ("seq", "kv"), [(i, i ^ mask) for i in range(count)])
        source = ((2 * side + core) ^ (mask & 1) * 2 ^ (mask >> 1)) * size
        out_doc = lax.dynamic_update_slice(out_doc, got, (0, source))
    return out_band, out_doc


def plain_program(
    q_band, k_band, v_band, sink_band, q_doc, k_doc, v_doc, sink_doc, doc_starts, source_lists
):
    rows = q_band.shape[0]
    heads = k_band.shape[1] // HD
    shard = lax.axis_index("seq")

    def place(*dists):
        return jnp.stack([shard, 0, 0, 0, *dists]).astype(jnp.int32)

    rim = jnp.concatenate([k_band[rows - WIN :], v_band[rows - WIN :]], axis=1)
    rim = shifted(rim, 1)
    unit = jnp.concatenate([k_doc, v_doc], axis=1)
    units = [unit] + [shifted(unit, d) for d in range(1, BACK + 1)]
    band = band_call(
        place(), doc_starts, sink_band, q_band, k_band, v_band, rim, heads, rows, False, None
    )[0]
    plan = DocPlan(True, True, 1, heads, 0, BACK + 1, rows, False)
    doc = doc_call(
        plan, place(*range(BACK + 1)), doc_starts, source_lists, sink_doc, None,
        (q_doc,), units, None, None,
    )[0]
    return relay(band), relay(doc)


def solution(mesh):
    placed = (
        P("seq", "kv"),
        P("seq", "kv"),
        P("seq", "kv"),
        P("kv"),
        P("seq", "kv"),
        P("seq", "kv"),
        P("seq", "kv"),
        P("kv"),
        P(),
        P("seq", None),
    )

    def per_device(*args):
        heads = args[1].shape[1] // HD
        even = heads % 4 == 0 and mesh.shape["kv"] == 2 and mesh.shape["seq"] % 4 == 0
        return (paired_program if even else plain_program)(*args)

    return jax.shard_map(
        per_device,
        mesh=mesh,
        in_specs=placed,
        out_specs=(P(("seq", "kv"), None), P(("seq", "kv"), None)),
        check_vma=False,
    )
```

```python
import functools
import jax
import jax.numpy as jnp
from jax import lax
from jax.experimental import pallas as pl
from jax.experimental.pallas import tpu as pltpu
from jax.sharding import PartitionSpec as P

HD = 64
G = 8
WIN = 128
BACK = 8
LOG2E = 1.4426950408889634
SCORE_SCALE = HD ** (-0.5) * LOG2E
NEG = -1e30
SAFE_TOTAL = 2.0**100
NEVER = 2**30
FEATURES = 128
SHARD_LANE = 64
CUT = 2.0**15
TALL = HD + 16
PARAMS = pltpu.CompilerParams(
    dimension_semantics=("arbitrary",), vmem_limit_bytes=48 * 1024 * 1024
)


def interval_rows(starts_ref):
    lane = lax.broadcasted_iota(jnp.int32, (8, FEATURES), 1)
    begin = jnp.full((8, FEATURES), NEVER, jnp.int32)
    end = begin
    for i in range(starts_ref.shape[0]):
        entry = starts_ref[i]
        begin = jnp.where(lane == i, entry, begin)
        end = jnp.where(lane == i - 1, entry, end)
    return begin, end


def key_features(starts_ref, low, shard, rows):
    begin, end = interval_rows(starts_ref)
    u = low + lax.broadcasted_iota(jnp.int32, (rows, FEATURES), 0)
    lane = lax.broadcasted_iota(jnp.int32, (rows, FEATURES), 1)
    own = jnp.where(shard < 0, SHARD_LANE - 1, SHARD_LANE + shard)
    marked = (lane == own) | ((u >= begin[:1]) & (u < end[:1]))
    return jnp.where(marked, 1.0, 0.0).astype(jnp.bfloat16)


def query_features(starts_ref, low, named, rows):
    begin, end = (x.T[:, :1] for x in interval_rows(starts_ref))
    t = low + lax.broadcasted_iota(jnp.int32, (FEATURES, rows), 1)
    row = lax.broadcasted_iota(jnp.int32, (FEATURES, rows), 0)
    seen = (t >= begin) & (t < end) & (row < SHARD_LANE)
    for shard in named:
        seen = seen | ((row == SHARD_LANE + shard) & (shard >= 0))
    return jnp.where(seen, 0.0, -CUT).astype(jnp.bfloat16)


def score(key_block, query_cols):
    return jnp.dot(key_block, query_cols, preferred_element_type=jnp.float32) * SCORE_SCALE


def plain_weights(key_block, query_cols, bias=None):
    scores = score(key_block, query_cols)
    if bias is not None:
        scores = scores + bias
    return jnp.exp2(scores).astype(jnp.bfloat16)


def weigh(value_rows, weight):
    return jnp.dot(value_rows, weight, preferred_element_type=jnp.float32)


def topped(state, key_block, query_cols, value_rows, bias=None):
    top, acc = state
    scores = score(key_block, query_cols)
    if bias is not None:
        scores = scores + bias
    new_top = jnp.maximum(top, jnp.max(scores, axis=0, keepdims=True))
    weight = jnp.exp2(scores - new_top).astype(jnp.bfloat16)
    return new_top, acc * jnp.exp2(top - new_top) + weigh(value_rows, weight)


def fresh(total):
    row = lax.broadcasted_iota(jnp.int32, (TALL, total.shape[1]), 0)
    return jnp.where(row == HD, total, 0.0)


def slotted(col, head, heads):
    if heads == 1:
        return col
    empty = jnp.zeros_like(col)
    return jnp.concatenate([jnp.where(head == i, col, empty) for i in range(heads)], axis=0)


def overflowed(total):
    return jnp.max(jnp.where(total <= SAFE_TOTAL, 0.0, 1.0)) > 0.5


def sink_lanes(sink_ref, first, count, rows):
    return jnp.concatenate(
        [jnp.full((1, rows), sink_ref[first + e] * LOG2E, jnp.float32) for e in range(count)], axis=1
    )


class DocPlan:
    def __init__(self, first, last, grp, heads, earlier, units, rows, pieces, wide=4):
        self.first, self.last, self.grp, self.heads = first, last, grp, heads
        self.earlier, self.units, self.rows, self.pieces = earlier, units, rows, pieces
        self.wide = wide


def doc_body(plan, *refs):
    first, last, grp, heads, rows = plan.first, plan.last, plan.grp, plan.heads, plan.rows
    wide = plan.wide
    count = plan.earlier + plan.units
    refs = list(refs)
    where_ref, starts_ref, sink_ref = refs[:3]
    del refs[:3]
    list_refs = [refs.pop(0) for _ in range(grp)]
    query_refs = [refs.pop(0) for _ in range(grp)]
    unit_refs = [refs.pop(0) for _ in range(count)]
    if not first:
        acc_in = refs.pop(0)
    if last:
        piece_refs = [refs.pop(0) for _ in range(2 * grp if plan.pieces else 1)]
    else:
        acc_out = refs.pop(0)
    value_ref, key_ref, bias_ref, acc_ref, cols_ref = refs
    step = pl.program_id(0)
    core = where_ref[1]
    lowest = where_ref[0] - core
    width = heads * HD
    part = wide * rows
    lanes = grp * part
    new = range(plan.earlier, count)
    own = 0 if first or plan.earlier else -1

    def set_unit(n):
        unit = unit_refs[n][...]
        turned = unit[:, width:].T if width % 128 == 0 else unit.T[width:]
        for i in range(heads):
            value_ref[n, i, :HD] = turned[i * HD : (i + 1) * HD]
            value_ref[n, i, HD:] = jnp.ones((TALL - HD, grp * rows), jnp.bfloat16)
        key_ref[n, :, FEATURES:] = unit[:, :width]
        for r in range(grp):
            shard = lowest + (r ^ core) - where_ref[4 + n] if grp > 1 else lowest - where_ref[4 + n]
            marks = key_features(starts_ref, shard * rows, shard, rows)
            key_ref[n, r * rows : (r + 1) * rows, :FEATURES] = marks

    @pl.when(step == 0)
    def _():
        for n in new:
            set_unit(n)
        for a in range(grp):
            entries = [list_refs[0][0, i] for i in range(BACK)]
            if grp == 2:
                entries = [jnp.where(core == a, x, list_refs[1][0, i]) for i, x in enumerate(entries)]
            named = [lowest + a] + entries
            marks = query_features(starts_ref, (lowest + a) * rows, named, rows)
            for e in range(wide):
                spot = slice(a * part + e * rows, a * part + (e + 1) * rows)
                cols_ref[:FEATURES, spot] = marks
        if own == 0:
            u = lax.broadcasted_iota(jnp.int32, (rows, part), 0)
            t = jnp.bitwise_and(lax.broadcasted_iota(jnp.int32, (rows, part), 1), rows - 1)
            bias_ref[...] = jnp.where(u <= t, 0.0, NEG)

    head = step // (G // wide)
    sinks = sink_lanes(sink_ref, core * heads * G + wide * step, wide, rows)
    sinks = jnp.concatenate([sinks] * grp, axis=1)
    for a in range(grp):
        query = query_refs[0][...]
        if grp == 2:
            query = jnp.where(core == a, query, query_refs[1][...])
        turned = query.T
        for e in range(wide):
            spot = slice(a * part + e * rows, a * part + (e + 1) * rows)
            cols_ref[FEATURES:, spot] = slotted(turned[e * HD : (e + 1) * HD], head, heads)

    def own_span(r):
        return slice(0, rows) if grp == 1 else pl.ds(pl.multiple_of((r ^ core) * rows, rows), rows)

    def own_pairs():
        pairs = [(r, slice(r * part, (r + 1) * part), bias_ref[...]) for r in range(grp)]
        return pairs + ([(0, slice(part, lanes), None)] if grp == 2 else [])

    def rows_of(n):
        return [slice(r * rows, (r + 1) * rows) for r in range(grp)]

    gain = fresh(jnp.exp2(sinks)) if first else acc_in[0]
    gains = [gain[:, a * part : (a + 1) * part] for a in range(grp)]
    for n in new:
        if n == own:
            for r, span, bias in own_pairs():
                weight = plain_weights(key_ref[n, own_span(r)], cols_ref[:, span], bias)
                a = span.start // part
                gains[a] = gains[a] + weigh(value_ref[n, head, :, own_span(r)], weight)
            continue
        for a in range(grp):
            cols = cols_ref[:, a * part : (a + 1) * part]
            weights = [plain_weights(key_ref[n, span], cols) for span in rows_of(n)]
            gains[a] = gains[a] + weigh(value_ref[n, head], jnp.concatenate(weights, axis=0))
    for a in range(grp):
        acc_ref[:, a * part : (a + 1) * part] = gains[a]

    if not last:
        acc_out[0] = acc_ref[...]
        return

    @pl.when(overflowed(acc_ref[HD : HD + 1]))
    def _():
        for n in range(plan.earlier):
            set_unit(n)
        for a in range(grp):
            spot = slice(a * part, (a + 1) * part)
            state = sinks[:, spot], fresh(jnp.ones((1, part), jnp.float32))
            for r, span, bias in own_pairs():
                if span.start == a * part:
                    values = value_ref[0, head, :, own_span(r)]
                    state = topped(state, key_ref[0, own_span(r)], cols_ref[:, spot], values, bias)
            for n in range(1, count):
                for span in rows_of(n):
                    values = value_ref[n, head, :, span]
                    state = topped(state, key_ref[n, span], cols_ref[:, spot], values)
            acc_ref[:, spot] = state[1]

    result = acc_ref[:HD] * (1.0 / acc_ref[HD : HD + 1])
    blocks = []
    for a in range(grp):
        parts = [result[:, a * part + e * rows : a * part + (e + 1) * rows] for e in range(wide)]
        blocks.append(jnp.concatenate(parts, axis=0).T.astype(jnp.bfloat16))
    if not plan.pieces:
        piece_refs[0][...] = blocks[0]
        return
    half = rows // 2
    side = where_ref[2]
    for a in range(grp):
        block = jnp.where(core == a, blocks[0], blocks[1])
        low, high = block[:half], block[half:]
        piece_refs[2 * a][...] = jnp.where(side == 0, low, high)
        piece_refs[2 * a + 1][...] = jnp.where(side == 0, high, low)


def doc_call(plan, where, starts, sinks, lists, queries, units, state, columns):
    grp, heads, rows, wide = plan.grp, plan.heads, plan.rows, plan.wide
    steps = heads * G // wide
    size = wide * HD
    width = heads * HD
    count = plan.earlier + plan.units
    smem = pl.BlockSpec(memory_space=pltpu.SMEM)
    args = [where, starts, sinks, *lists]
    specs = [smem] * (2 + grp)
    args += list(queries)
    specs.append(pl.BlockSpec((rows, size), lambda j, w: (0, w[1] * steps + j)))
    if grp == 2:
        specs.append(pl.BlockSpec((rows, size), lambda j, w: (0, j)))
    for unit in units:
        args.append(unit)
        specs.append(pl.BlockSpec((grp * rows, 2 * width), lambda j, w: (0, 0)))
    lanes = wide * grp * rows
    state_spec = pl.BlockSpec((1, TALL, lanes), lambda j, w: (j, 0, 0))
    aliases = {}
    if not plan.first:
        if not plan.last:
            aliases = {len(args): 0}
        args.append(state)
        specs.append(state_spec)
    if not plan.last:
        out_shape = [jax.ShapeDtypeStruct((steps, TALL, lanes), jnp.float32)]
        out_specs = [state_spec]
    elif plan.pieces:
        half = rows // 2
        out_shape = [jax.ShapeDtypeStruct((half, columns), jnp.bfloat16)]
        out_specs = [pl.BlockSpec((half, size), lambda j, w: (0, w[3] * steps + j))]
        for _ in range(2 * grp - 1):
            out_shape.append(jax.ShapeDtypeStruct((half, steps * size), jnp.bfloat16))
            out_specs.append(pl.BlockSpec((half, size), lambda j, w: (0, j)))
    else:
        out_shape = [jax.ShapeDtypeStruct((rows, steps * size), jnp.bfloat16)]
        out_specs = [pl.BlockSpec((rows, size), lambda j, w: (0, j))]
    return pl.pallas_call(
        functools.partial(doc_body, plan),
        out_shape=out_shape,
        grid_spec=pltpu.PrefetchScalarGridSpec(
            num_scalar_prefetch=1,
            grid=(steps,),
            in_specs=specs,
            out_specs=out_specs,
            scratch_shapes=[
                pltpu.VMEM((count, heads, TALL, grp * rows), jnp.bfloat16),
                pltpu.VMEM((count, grp * rows, FEATURES + width), jnp.bfloat16),
                pltpu.VMEM((rows, wide * rows), jnp.float32),
                pltpu.VMEM((TALL, lanes), jnp.float32),
                pltpu.VMEM((FEATURES + width, lanes), jnp.bfloat16),
            ],
        ),
        input_output_aliases=aliases,
        compiler_params=PARAMS,
        name="doc_attention",
    )(*args)


def band_body(heads, rows, wide, pieces, where_ref, starts_ref, sink_ref, query_ref, key_ref, value_ref, rim_ref, *refs):
    out_refs, (keys, values, bias_ref, cols_ref, acc_ref) = refs[:-5], refs[-5:]
    step = pl.program_id(0)
    width = heads * HD
    low = where_ref[0] * rows
    tiles = rows // WIN
    lanes = wide * WIN

    @pl.when(step == 0)
    def _():
        rim = rim_ref[...]
        keys[:WIN, FEATURES:] = rim[:, :width]
        keys[WIN:, FEATURES:] = key_ref[...]
        shard = where_ref[0]
        keys[:WIN, :FEATURES] = key_features(starts_ref, low - WIN, shard - 1, WIN)
        keys[WIN:, :FEATURES] = key_features(starts_ref, low, shard, rows)
        turned_rim = rim[:, width:].T if width % 128 == 0 else rim.T[width:]
        turned_own = value_ref[...].T
        for i in range(heads):
            values[i, :HD, :WIN] = turned_rim[i * HD : (i + 1) * HD]
            values[i, :HD, WIN:] = turned_own[i * HD : (i + 1) * HD]
            values[i, HD:] = jnp.ones((TALL - HD, rows + WIN), jnp.bfloat16)
        marks = query_features(starts_ref, low, [shard, shard - 1], rows)
        for tile in range(tiles):
            for e in range(wide):
                cols_ref[tile, :FEATURES, e * WIN : (e + 1) * WIN] = marks[:, tile * WIN : (tile + 1) * WIN]
        u = lax.broadcasted_iota(jnp.int32, (2 * WIN, lanes), 0)
        t = jnp.bitwise_and(lax.broadcasted_iota(jnp.int32, (2 * WIN, lanes), 1), WIN - 1)
        bias_ref[...] = jnp.where((u <= t + WIN) & (u > t), 0.0, NEG)

    head = step // (G // wide)
    turned = query_ref[...].T
    sinks = sink_lanes(sink_ref, wide * step, wide, WIN)

    for tile in range(tiles):
        span = slice(tile * WIN, (tile + 1) * WIN)
        for e in range(wide):
            col = slotted(turned[e * HD : (e + 1) * HD, span], head, heads)
            cols_ref[tile, FEATURES:, e * WIN : (e + 1) * WIN] = col
    for tile in range(tiles):
        span = slice(tile * WIN, (tile + 2) * WIN)
        weight = plain_weights(keys[span], cols_ref[tile], bias_ref[...])
        acc_ref[tile] = fresh(jnp.exp2(sinks)) + weigh(values[head, :, span], weight)

    @pl.when(overflowed(acc_ref[:, HD : HD + 1]))
    def _():
        for tile in range(tiles):
            span = slice(tile * WIN, (tile + 2) * WIN)
            state = sinks, fresh(jnp.ones((1, lanes), jnp.float32))
            state = topped(state, keys[span], cols_ref[tile], values[head, :, span], bias_ref[...])
            acc_ref[tile] = state[1]

    finished = []
    for tile in range(tiles):
        result = acc_ref[tile, :HD] * (1.0 / acc_ref[tile, HD : HD + 1])
        parts = [result[:, e * WIN : (e + 1) * WIN] for e in range(wide)]
        finished.append(jnp.concatenate(parts, axis=0).T.astype(jnp.bfloat16))
    if pieces:
        side = where_ref[2]
        out_refs[0][...] = jnp.where(side == 0, finished[0], finished[1])
        out_refs[1][...] = jnp.where(side == 0, finished[1], finished[0])
    else:
        for tile, value in enumerate(finished):
            out_refs[0][tile * WIN : (tile + 1) * WIN] = value


def band_call(where, starts, sinks, queries, keys, value_rows, rim, heads, rows, pieces, columns):
    wide = 4
    steps = heads * G // wide
    size = wide * HD
    width = heads * HD
    tiles = rows // WIN
    smem = pl.BlockSpec(memory_space=pltpu.SMEM)
    if pieces:
        out_shape = [
            jax.ShapeDtypeStruct((WIN, columns), jnp.bfloat16),
            jax.ShapeDtypeStruct((WIN, steps * size), jnp.bfloat16),
        ]
        out_specs = [
            pl.BlockSpec((WIN, size), lambda j, w: (0, w[2] * steps + j)),
            pl.BlockSpec((WIN, size), lambda j, w: (0, j)),
        ]
    else:
        out_shape = [jax.ShapeDtypeStruct((rows, steps * size), jnp.bfloat16)]
        out_specs = [pl.BlockSpec((rows, size), lambda j, w: (0, j))]

    def fixed(j, w):
        return (0, 0)

    return pl.pallas_call(
        functools.partial(band_body, heads, rows, wide, pieces),
        out_shape=out_shape,
        grid_spec=pltpu.PrefetchScalarGridSpec(
            num_scalar_prefetch=1,
            grid=(steps,),
            in_specs=[
                smem,
                smem,
                pl.BlockSpec((rows, size), lambda j, w: (0, j)),
                pl.BlockSpec((rows, width), fixed),
                pl.BlockSpec((rows, width), fixed),
                pl.BlockSpec((WIN, 2 * width), fixed),
            ],
            out_specs=out_specs,
            scratch_shapes=[
                pltpu.VMEM((rows + WIN, FEATURES + width), jnp.bfloat16),
                pltpu.VMEM((heads, TALL, rows + WIN), jnp.bfloat16),
                pltpu.VMEM((2 * WIN, wide * WIN), jnp.float32),
                pltpu.VMEM((tiles, FEATURES + width, wide * WIN), jnp.bfloat16),
                pltpu.VMEM((tiles, TALL, wide * WIN), jnp.float32),
            ],
        ),
        compiler_params=PARAMS,
        name="band_attention",
    )(where, starts, sinks, queries, keys, value_rows, rim)


def shifted(value, steps):
    count = lax.axis_size("seq")
    return lax.ppermute(value, "seq", [(i, i + steps) for i in range(count - steps)])


def swapped(value, bit):
    count = lax.axis_size("seq")
    return lax.ppermute(value, "seq", [(i, i ^ bit) for i in range(count)])


def relay(result):
    return lax.all_to_all(result, "kv", split_axis=0, concat_axis=1, tiled=True)


def paired_program(
    q_band, k_band, v_band, sink_band, q_doc, k_doc, v_doc, sink_doc, doc_starts, source_lists
):
    rows = q_band.shape[0]
    heads = k_band.shape[1] // HD
    mine = heads // 2
    width = mine * HD
    columns = 2 * q_band.shape[1]
    shard, side = lax.axis_index("seq"), lax.axis_index("kv")
    core = shard % 2
    layer = shard // 2 % 2
    flip = 4 * layer - 2

    def place(*dists):
        return jnp.stack([shard, core, side, 2 * side + core, *dists]).astype(jnp.int32)

    def half(value, which, size):
        return lax.dynamic_slice_in_dim(value, which * size, size, axis=1)

    away = jnp.concatenate([half(k_doc, 1 - core, width), half(v_doc, 1 - core, width)], axis=1)
    near = swapped(away, 1)
    rim = jnp.concatenate([k_band[rows - WIN :], v_band[rows - WIN :]], axis=1)
    rim = shifted(rim, 1)
    kept = jnp.concatenate([half(k_doc, core, width), half(v_doc, core, width)], axis=1)
    unit = jnp.concatenate([kept, near], axis=0)
    back4 = shifted(unit, 4)
    back8 = shifted(unit, 8)
    q_later, _ = lax.optimization_barrier((q_doc, unit))
    mate_lists = swapped(source_lists, 1)
    q_mate = swapped(half(q_later, 1 - core, mine * G * HD), 1)
    cross4 = swapped(back4, 2)
    late = swapped(jnp.where(layer == 0, unit, back8), 2)
    band_out, band_send = band_call(
        place(), doc_starts, sink_band, q_band, k_band, v_band, rim, heads, rows, True, columns
    )
    band_got = lax.ppermute(band_send, "kv", [(0, 1), (1, 0)])
    out_band = lax.dynamic_update_slice(band_out, band_got, (0, (1 - side) * q_band.shape[1]))

    def doc(first, last, units, dists, earlier, state):
        plan = DocPlan(first, last, 2, mine, earlier, len(units) - earlier, rows, True)
        return doc_call(
            plan, place(*dists), doc_starts, sink_doc, (source_lists, mate_lists),
            (q_doc, q_mate), units, state, columns,
        )

    units = [unit, back4, cross4, back8, late]
    dists = [0, 4, 4 + flip, 8, jnp.where(layer == 0, 6, 2)]
    (state,) = doc(True, False, units[:2], dists[:2], 0, None)
    (state,) = doc(False, False, units[2:4], dists[2:4], 0, state)
    out_doc, *sends = doc(False, True, units, dists, 4, state)
    size = mine * G * HD
    for mask, send in zip((1, 2, 3), sends):
        count = 2 * lax.axis_size("seq")
        got = lax.ppermute(send, ("seq", "kv"), [(i, i ^ mask) for i in range(count)])
        source = ((2 * side + core) ^ (mask & 1) * 2 ^ (mask >> 1)) * size
        out_doc = lax.dynamic_update_slice(out_doc, got, (0, source))
    return out_band, out_doc


def plain_program(
    q_band, k_band, v_band, sink_band, q_doc, k_doc, v_doc, sink_doc, doc_starts, source_lists
):
    rows = q_band.shape[0]
    heads = k_band.shape[1] // HD
    shard = lax.axis_index("seq")

    def place(*dists):
        return jnp.stack([shard, 0, 0, 0, *dists]).astype(jnp.int32)

    rim = jnp.concatenate([k_band[rows - WIN :], v_band[rows - WIN :]], axis=1)
    rim = shifted(rim, 1)
    unit = jnp.concatenate([k_doc, v_doc], axis=1)
    units = [unit] + [shifted(unit, d) for d in range(1, BACK + 1)]
    band = band_call(
        place(), doc_starts, sink_band, q_band, k_band, v_band, rim, heads, rows, False, None
    )[0]
    plan = DocPlan(True, True, 1, heads, 0, BACK + 1, rows, False)
    doc = doc_call(
        plan, place(*range(BACK + 1)), doc_starts, sink_doc, (source_lists,),
        (q_doc,), units, None, None,
    )[0]
    return relay(band), relay(doc)


def solution(mesh):
    placed = (
        P("seq", "kv"),
        P("seq", "kv"),
        P("seq", "kv"),
        P("kv"),
        P("seq", "kv"),
        P("seq", "kv"),
        P("seq", "kv"),
        P("kv"),
        P(),
        P("seq", None),
    )

    def per_device(*args):
        heads = args[1].shape[1] // HD
        even = heads % 4 == 0 and mesh.shape["kv"] == 2 and mesh.shape["seq"] % 4 == 0
        return (paired_program if even else plain_program)(*args)

    return jax.shard_map(
        per_device,
        mesh=mesh,
        in_specs=placed,
        out_specs=(P(("seq", "kv"), None), P(("seq", "kv"), None)),
        check_vma=False,
    )
```

```python
import functools
import jax
import jax.numpy as jnp
from jax import lax
from jax.experimental import pallas as pl
from jax.experimental.pallas import tpu as pltpu
from jax.sharding import PartitionSpec as P

HD = 64
G = 8
WIN = 128
BACK = 8
LOG2E = 1.4426950408889634
SCORE_SCALE = HD ** (-0.5) * LOG2E
NEG = -1e30
SAFE_TOTAL = 2.0**100
NEVER = 2**30
FEATURES = 128
SHARD_LANE = 64
CUT = 2.0**15
TALL = HD + 16
PARAMS = pltpu.CompilerParams(
    dimension_semantics=("arbitrary",), vmem_limit_bytes=48 * 1024 * 1024
)


def interval_rows(starts_ref):
    lane = lax.broadcasted_iota(jnp.int32, (8, FEATURES), 1)
    begin = jnp.full((8, FEATURES), NEVER, jnp.int32)
    end = begin
    for i in range(starts_ref.shape[0]):
        entry = starts_ref[i]
        begin = jnp.where(lane == i, entry, begin)
        end = jnp.where(lane == i - 1, entry, end)
    return begin, end


def key_features(starts_ref, low, shard, rows):
    begin, end = interval_rows(starts_ref)
    u = low + lax.broadcasted_iota(jnp.int32, (rows, FEATURES), 0)
    lane = lax.broadcasted_iota(jnp.int32, (rows, FEATURES), 1)
    own = jnp.where(shard < 0, SHARD_LANE - 1, SHARD_LANE + shard)
    marked = (lane == own) | ((u >= begin[:1]) & (u < end[:1]))
    return jnp.where(marked, 1.0, 0.0).astype(jnp.bfloat16)


def query_features(starts_ref, low, named, rows):
    begin, end = (x.T[:, :1] for x in interval_rows(starts_ref))
    t = low + lax.broadcasted_iota(jnp.int32, (FEATURES, rows), 1)
    row = lax.broadcasted_iota(jnp.int32, (FEATURES, rows), 0)
    seen = (t >= begin) & (t < end) & (row < SHARD_LANE)
    for shard in named:
        seen = seen | ((row == SHARD_LANE + shard) & (shard >= 0))
    return jnp.where(seen, 0.0, -CUT).astype(jnp.bfloat16)


def score(key_block, query_cols):
    return jnp.dot(key_block, query_cols, preferred_element_type=jnp.float32) * SCORE_SCALE


def plain_weights(key_block, query_cols, bias=None):
    scores = score(key_block, query_cols)
    if bias is not None:
        scores = scores + bias
    return jnp.exp2(scores).astype(jnp.bfloat16)


def weigh(value_rows, weight):
    return jnp.dot(value_rows, weight, preferred_element_type=jnp.float32)


def topped(state, key_block, query_cols, value_rows, bias=None):
    top, acc = state
    scores = score(key_block, query_cols)
    if bias is not None:
        scores = scores + bias
    new_top = jnp.maximum(top, jnp.max(scores, axis=0, keepdims=True))
    weight = jnp.exp2(scores - new_top).astype(jnp.bfloat16)
    return new_top, acc * jnp.exp2(top - new_top) + weigh(value_rows, weight)


def fresh(total):
    row = lax.broadcasted_iota(jnp.int32, (TALL, total.shape[1]), 0)
    return jnp.where(row == HD, total, 0.0)


def slotted(col, head, heads):
    if heads == 1:
        return col
    empty = jnp.zeros_like(col)
    return jnp.concatenate([jnp.where(head == i, col, empty) for i in range(heads)], axis=0)


def overflowed(total):
    return jnp.max(jnp.where(total <= SAFE_TOTAL, 0.0, 1.0)) > 0.5


def sink_lanes(sink_ref, first, count, rows):
    return jnp.concatenate(
        [jnp.full((1, rows), sink_ref[first + e] * LOG2E, jnp.float32) for e in range(count)], axis=1
    )


class DocPlan:
    def __init__(self, first, last, grp, heads, earlier, units, rows, pieces, wide=8):
        self.first, self.last, self.grp, self.heads = first, last, grp, heads
        self.earlier, self.units, self.rows, self.pieces = earlier, units, rows, pieces
        self.wide = wide


def doc_body(plan, *refs):
    first, last, grp, heads, rows = plan.first, plan.last, plan.grp, plan.heads, plan.rows
    wide = plan.wide
    count = plan.earlier + plan.units
    refs = list(refs)
    where_ref, starts_ref, sink_ref = refs[:3]
    del refs[:3]
    list_refs = [refs.pop(0) for _ in range(grp)]
    query_refs = [refs.pop(0) for _ in range(grp)]
    unit_refs = [refs.pop(0) for _ in range(count)]
    if not first:
        acc_in = refs.pop(0)
    if last:
        piece_refs = [refs.pop(0) for _ in range(2 * grp if plan.pieces else 1)]
    else:
        acc_out = refs.pop(0)
    value_ref, key_ref, bias_ref, acc_ref, cols_ref = refs
    step = pl.program_id(0)
    core = where_ref[1]
    lowest = where_ref[0] - core
    width = heads * HD
    part = wide * rows
    lanes = grp * part
    new = range(plan.earlier, count)
    own = 0 if first or plan.earlier else -1

    def set_unit(n):
        unit = unit_refs[n][...]
        turned = unit[:, width:].T if width % 128 == 0 else unit.T[width:]
        for i in range(heads):
            value_ref[n, i, :HD] = turned[i * HD : (i + 1) * HD]
            value_ref[n, i, HD:] = jnp.ones((TALL - HD, grp * rows), jnp.bfloat16)
        key_ref[n, :, FEATURES:] = unit[:, :width]
        for r in range(grp):
            shard = lowest + (r ^ core) - where_ref[4 + n] if grp > 1 else lowest - where_ref[4 + n]
            marks = key_features(starts_ref, shard * rows, shard, rows)
            key_ref[n, r * rows : (r + 1) * rows, :FEATURES] = marks

    @pl.when(step == 0)
    def _():
        for n in new:
            set_unit(n)
        for a in range(grp):
            entries = [list_refs[0][0, i] for i in range(BACK)]
            if grp == 2:
                entries = [jnp.where(core == a, x, list_refs[1][0, i]) for i, x in enumerate(entries)]
            named = [lowest + a] + entries
            marks = query_features(starts_ref, (lowest + a) * rows, named, rows)
            for e in range(wide):
                spot = slice(a * part + e * rows, a * part + (e + 1) * rows)
                cols_ref[:FEATURES, spot] = marks
        if own == 0:
            u = lax.broadcasted_iota(jnp.int32, (rows, part), 0)
            t = jnp.bitwise_and(lax.broadcasted_iota(jnp.int32, (rows, part), 1), rows - 1)
            bias_ref[...] = jnp.where(u <= t, 0.0, NEG)

    head = step // (G // wide)
    sinks = sink_lanes(sink_ref, core * heads * G + wide * step, wide, rows)
    sinks = jnp.concatenate([sinks] * grp, axis=1)
    for a in range(grp):
        query = query_refs[0][...]
        if grp == 2:
            query = jnp.where(core == a, query, query_refs[1][...])
        turned = query.T
        for e in range(wide):
            spot = slice(a * part + e * rows, a * part + (e + 1) * rows)
            cols_ref[FEATURES:, spot] = slotted(turned[e * HD : (e + 1) * HD], head, heads)

    def own_span(r):
        return slice(0, rows) if grp == 1 else pl.ds(pl.multiple_of((r ^ core) * rows, rows), rows)

    def own_pairs():
        pairs = [(r, slice(r * part, (r + 1) * part), bias_ref[...]) for r in range(grp)]
        return pairs + ([(0, slice(part, lanes), None)] if grp == 2 else [])

    def rows_of(n):
        return [slice(r * rows, (r + 1) * rows) for r in range(grp)]

    gain = fresh(jnp.exp2(sinks)) if first else acc_in[0]
    gains = [gain[:, a * part : (a + 1) * part] for a in range(grp)]
    for n in new:
        if n == own:
            for r, span, bias in own_pairs():
                weight = plain_weights(key_ref[n, own_span(r)], cols_ref[:, span], bias)
                a = span.start // part
                gains[a] = gains[a] + weigh(value_ref[n, head, :, own_span(r)], weight)
            continue
        for a in range(grp):
            cols = cols_ref[:, a * part : (a + 1) * part]
            weights = [plain_weights(key_ref[n, span], cols) for span in rows_of(n)]
            gains[a] = gains[a] + weigh(value_ref[n, head], jnp.concatenate(weights, axis=0))
    for a in range(grp):
        acc_ref[:, a * part : (a + 1) * part] = gains[a]

    if not last:
        acc_out[0] = acc_ref[...]
        return

    @pl.when(overflowed(acc_ref[HD : HD + 1]))
    def _():
        for n in range(plan.earlier):
            set_unit(n)
        for a in range(grp):
            spot = slice(a * part, (a + 1) * part)
            state = sinks[:, spot], fresh(jnp.ones((1, part), jnp.float32))
            for r, span, bias in own_pairs():
                if span.start == a * part:
                    values = value_ref[0, head, :, own_span(r)]
                    state = topped(state, key_ref[0, own_span(r)], cols_ref[:, spot], values, bias)
            for n in range(1, count):
                for span in rows_of(n):
                    values = value_ref[n, head, :, span]
                    state = topped(state, key_ref[n, span], cols_ref[:, spot], values)
            acc_ref[:, spot] = state[1]

    result = acc_ref[:HD] * (1.0 / acc_ref[HD : HD + 1])
    blocks = []
    for a in range(grp):
        parts = [result[:, a * part + e * rows : a * part + (e + 1) * rows] for e in range(wide)]
        blocks.append(jnp.concatenate(parts, axis=0).T.astype(jnp.bfloat16))
    if not plan.pieces:
        piece_refs[0][...] = blocks[0]
        return
    half = rows // 2
    side = where_ref[2]
    for a in range(grp):
        block = jnp.where(core == a, blocks[0], blocks[1])
        low, high = block[:half], block[half:]
        piece_refs[2 * a][...] = jnp.where(side == 0, low, high)
        piece_refs[2 * a + 1][...] = jnp.where(side == 0, high, low)


def doc_call(plan, where, starts, sinks, lists, queries, units, state, columns):
    grp, heads, rows, wide = plan.grp, plan.heads, plan.rows, plan.wide
    steps = heads * G // wide
    size = wide * HD
    width = heads * HD
    count = plan.earlier + plan.units
    smem = pl.BlockSpec(memory_space=pltpu.SMEM)
    args = [where, starts, sinks, *lists]
    specs = [smem] * (2 + grp)
    args += list(queries)
    specs.append(pl.BlockSpec((rows, size), lambda j, w: (0, w[1] * steps + j)))
    if grp == 2:
        specs.append(pl.BlockSpec((rows, size), lambda j, w: (0, j)))
    for unit in units:
        args.append(unit)
        specs.append(pl.BlockSpec((grp * rows, 2 * width), lambda j, w: (0, 0)))
    lanes = wide * grp * rows
    state_spec = pl.BlockSpec((1, TALL, lanes), lambda j, w: (j, 0, 0))
    aliases = {}
    if not plan.first:
        if not plan.last:
            aliases = {len(args): 0}
        args.append(state)
        specs.append(state_spec)
    if not plan.last:
        out_shape = [jax.ShapeDtypeStruct((steps, TALL, lanes), jnp.float32)]
        out_specs = [state_spec]
    elif plan.pieces:
        half = rows // 2
        out_shape = [jax.ShapeDtypeStruct((half, columns), jnp.bfloat16)]
        out_specs = [pl.BlockSpec((half, size), lambda j, w: (0, w[3] * steps + j))]
        for _ in range(2 * grp - 1):
            out_shape.append(jax.ShapeDtypeStruct((half, steps * size), jnp.bfloat16))
            out_specs.append(pl.BlockSpec((half, size), lambda j, w: (0, j)))
    else:
        out_shape = [jax.ShapeDtypeStruct((rows, steps * size), jnp.bfloat16)]
        out_specs = [pl.BlockSpec((rows, size), lambda j, w: (0, j))]
    return pl.pallas_call(
        functools.partial(doc_body, plan),
        out_shape=out_shape,
        grid_spec=pltpu.PrefetchScalarGridSpec(
            num_scalar_prefetch=1,
            grid=(steps,),
            in_specs=specs,
            out_specs=out_specs,
            scratch_shapes=[
                pltpu.VMEM((count, heads, TALL, grp * rows), jnp.bfloat16),
                pltpu.VMEM((count, grp * rows, FEATURES + width), jnp.bfloat16),
                pltpu.VMEM((rows, wide * rows), jnp.float32),
                pltpu.VMEM((TALL, lanes), jnp.float32),
                pltpu.VMEM((FEATURES + width, lanes), jnp.bfloat16),
            ],
        ),
        input_output_aliases=aliases,
        compiler_params=PARAMS,
        name="doc_attention",
    )(*args)


def band_body(heads, rows, wide, pieces, where_ref, starts_ref, sink_ref, query_ref, key_ref, value_ref, rim_ref, *refs):
    out_refs, (keys, values, bias_ref, cols_ref, acc_ref) = refs[:-5], refs[-5:]
    step = pl.program_id(0)
    width = heads * HD
    low = where_ref[0] * rows
    tiles = rows // WIN
    lanes = wide * WIN

    @pl.when(step == 0)
    def _():
        rim = rim_ref[...]
        keys[:WIN, FEATURES:] = rim[:, :width]
        keys[WIN:, FEATURES:] = key_ref[...]
        shard = where_ref[0]
        keys[:WIN, :FEATURES] = key_features(starts_ref, low - WIN, shard - 1, WIN)
        keys[WIN:, :FEATURES] = key_features(starts_ref, low, shard, rows)
        turned_rim = rim[:, width:].T if width % 128 == 0 else rim.T[width:]
        turned_own = value_ref[...].T
        for i in range(heads):
            values[i, :HD, :WIN] = turned_rim[i * HD : (i + 1) * HD]
            values[i, :HD, WIN:] = turned_own[i * HD : (i + 1) * HD]
            values[i, HD:] = jnp.ones((TALL - HD, rows + WIN), jnp.bfloat16)
        marks = query_features(starts_ref, low, [shard, shard - 1], rows)
        for tile in range(tiles):
            for e in range(wide):
                cols_ref[tile, :FEATURES, e * WIN : (e + 1) * WIN] = marks[:, tile * WIN : (tile + 1) * WIN]
        u = lax.broadcasted_iota(jnp.int32, (2 * WIN, lanes), 0)
        t = jnp.bitwise_and(lax.broadcasted_iota(jnp.int32, (2 * WIN, lanes), 1), WIN - 1)
        bias_ref[...] = jnp.where((u <= t + WIN) & (u > t), 0.0, NEG)

    head = step // (G // wide)
    turned = query_ref[...].T
    sinks = sink_lanes(sink_ref, wide * step, wide, WIN)

    for tile in range(tiles):
        span = slice(tile * WIN, (tile + 1) * WIN)
        for e in range(wide):
            col = slotted(turned[e * HD : (e + 1) * HD, span], head, heads)
            cols_ref[tile, FEATURES:, e * WIN : (e + 1) * WIN] = col
    for tile in range(tiles):
        span = slice(tile * WIN, (tile + 2) * WIN)
        weight = plain_weights(keys[span], cols_ref[tile], bias_ref[...])
        acc_ref[tile] = fresh(jnp.exp2(sinks)) + weigh(values[head, :, span], weight)

    @pl.when(overflowed(acc_ref[:, HD : HD + 1]))
    def _():
        for tile in range(tiles):
            span = slice(tile * WIN, (tile + 2) * WIN)
            state = sinks, fresh(jnp.ones((1, lanes), jnp.float32))
            state = topped(state, keys[span], cols_ref[tile], values[head, :, span], bias_ref[...])
            acc_ref[tile] = state[1]

    finished = []
    for tile in range(tiles):
        result = acc_ref[tile, :HD] * (1.0 / acc_ref[tile, HD : HD + 1])
        parts = [result[:, e * WIN : (e + 1) * WIN] for e in range(wide)]
        finished.append(jnp.concatenate(parts, axis=0).T.astype(jnp.bfloat16))
    if pieces:
        side = where_ref[2]
        out_refs[0][...] = jnp.where(side == 0, finished[0], finished[1])
        out_refs[1][...] = jnp.where(side == 0, finished[1], finished[0])
    else:
        for tile, value in enumerate(finished):
            out_refs[0][tile * WIN : (tile + 1) * WIN] = value


def band_call(where, starts, sinks, queries, keys, value_rows, rim, heads, rows, pieces, columns):
    wide = 8
    steps = heads * G // wide
    size = wide * HD
    width = heads * HD
    tiles = rows // WIN
    smem = pl.BlockSpec(memory_space=pltpu.SMEM)
    if pieces:
        out_shape = [
            jax.ShapeDtypeStruct((WIN, columns), jnp.bfloat16),
            jax.ShapeDtypeStruct((WIN, steps * size), jnp.bfloat16),
        ]
        out_specs = [
            pl.BlockSpec((WIN, size), lambda j, w: (0, w[2] * steps + j)),
            pl.BlockSpec((WIN, size), lambda j, w: (0, j)),
        ]
    else:
        out_shape = [jax.ShapeDtypeStruct((rows, steps * size), jnp.bfloat16)]
        out_specs = [pl.BlockSpec((rows, size), lambda j, w: (0, j))]

    def fixed(j, w):
        return (0, 0)

    return pl.pallas_call(
        functools.partial(band_body, heads, rows, wide, pieces),
        out_shape=out_shape,
        grid_spec=pltpu.PrefetchScalarGridSpec(
            num_scalar_prefetch=1,
            grid=(steps,),
            in_specs=[
                smem,
                smem,
                pl.BlockSpec((rows, size), lambda j, w: (0, j)),
                pl.BlockSpec((rows, width), fixed),
                pl.BlockSpec((rows, width), fixed),
                pl.BlockSpec((WIN, 2 * width), fixed),
            ],
            out_specs=out_specs,
            scratch_shapes=[
                pltpu.VMEM((rows + WIN, FEATURES + width), jnp.bfloat16),
                pltpu.VMEM((heads, TALL, rows + WIN), jnp.bfloat16),
                pltpu.VMEM((2 * WIN, wide * WIN), jnp.float32),
                pltpu.VMEM((tiles, FEATURES + width, wide * WIN), jnp.bfloat16),
                pltpu.VMEM((tiles, TALL, wide * WIN), jnp.float32),
            ],
        ),
        compiler_params=PARAMS,
        name="band_attention",
    )(where, starts, sinks, queries, keys, value_rows, rim)


def shifted(value, steps):
    count = lax.axis_size("seq")
    return lax.ppermute(value, "seq", [(i, i + steps) for i in range(count - steps)])


def swapped(value, bit):
    count = lax.axis_size("seq")
    return lax.ppermute(value, "seq", [(i, i ^ bit) for i in range(count)])


def relay(result):
    return lax.all_to_all(result, "kv", split_axis=0, concat_axis=1, tiled=True)


def paired_program(
    q_band, k_band, v_band, sink_band, q_doc, k_doc, v_doc, sink_doc, doc_starts, source_lists
):
    rows = q_band.shape[0]
    heads = k_band.shape[1] // HD
    mine = heads // 2
    width = mine * HD
    columns = 2 * q_band.shape[1]
    shard, side = lax.axis_index("seq"), lax.axis_index("kv")
    core = shard % 2
    layer = shard // 2 % 2
    flip = 4 * layer - 2

    def place(*dists):
        return jnp.stack([shard, core, side, 2 * side + core, *dists]).astype(jnp.int32)

    def half(value, which, size):
        return lax.dynamic_slice_in_dim(value, which * size, size, axis=1)

    away = jnp.concatenate([half(k_doc, 1 - core, width), half(v_doc, 1 - core, width)], axis=1)
    away, mate_lists = lax.optimization_barrier((away, swapped(source_lists, 1)))
    near = swapped(away, 1)
    rim = jnp.concatenate([k_band[rows - WIN :], v_band[rows - WIN :]], axis=1)
    rim = shifted(rim, 1)
    kept = jnp.concatenate([half(k_doc, core, width), half(v_doc, core, width)], axis=1)
    unit = jnp.concatenate([kept, near], axis=0)
    back4 = shifted(unit, 4)
    back8 = shifted(unit, 8)
    q_later, _ = lax.optimization_barrier((q_doc, unit))
    q_mate = swapped(half(q_later, 1 - core, mine * G * HD), 1)
    cross4 = swapped(back4, 2)
    late = swapped(jnp.where(layer == 0, unit, back8), 2)
    band_out, band_send = band_call(
        place(), doc_starts, sink_band, q_band, k_band, v_band, rim, heads, rows, True, columns
    )
    band_got = lax.ppermute(band_send, "kv", [(0, 1), (1, 0)])
    out_band = lax.dynamic_update_slice(band_out, band_got, (0, (1 - side) * q_band.shape[1]))

    def doc(first, last, units, dists, earlier, state):
        plan = DocPlan(first, last, 2, mine, earlier, len(units) - earlier, rows, True)
        return doc_call(
            plan, place(*dists), doc_starts, sink_doc, (source_lists, mate_lists),
            (q_doc, q_mate), units, state, columns,
        )

    units = [unit, back4, cross4, back8, late]
    dists = [0, 4, 4 + flip, 8, jnp.where(layer == 0, 6, 2)]
    (state,) = doc(True, False, units[:2], dists[:2], 0, None)
    out_doc, *sends = doc(False, True, units, dists, 2, state)
    size = mine * G * HD
    for mask, send in zip((1, 2, 3), sends):
        count = 2 * lax.axis_size("seq")
        got = lax.ppermute(send, ("seq", "kv"), [(i, i ^ mask) for i in range(count)])
        source = ((2 * side + core) ^ (mask & 1) * 2 ^ (mask >> 1)) * size
        out_doc = lax.dynamic_update_slice(out_doc, got, (0, source))
    return out_band, out_doc


def plain_program(
    q_band, k_band, v_band, sink_band, q_doc, k_doc, v_doc, sink_doc, doc_starts, source_lists
):
    rows = q_band.shape[0]
    heads = k_band.shape[1] // HD
    shard = lax.axis_index("seq")

    def place(*dists):
        return jnp.stack([shard, 0, 0, 0, *dists]).astype(jnp.int32)

    rim = jnp.concatenate([k_band[rows - WIN :], v_band[rows - WIN :]], axis=1)
    rim = shifted(rim, 1)
    unit = jnp.concatenate([k_doc, v_doc], axis=1)
    units = [unit] + [shifted(unit, d) for d in range(1, BACK + 1)]
    band = band_call(
        place(), doc_starts, sink_band, q_band, k_band, v_band, rim, heads, rows, False, None
    )[0]
    plan = DocPlan(True, True, 1, heads, 0, BACK + 1, rows, False)
    doc = doc_call(
        plan, place(*range(BACK + 1)), doc_starts, sink_doc, (source_lists,),
        (q_doc,), units, None, None,
    )[0]
    return relay(band), relay(doc)


def solution(mesh):
    placed = (
        P("seq", "kv"),
        P("seq", "kv"),
        P("seq", "kv"),
        P("kv"),
        P("seq", "kv"),
        P("seq", "kv"),
        P("seq", "kv"),
        P("kv"),
        P(),
        P("seq", None),
    )

    def per_device(*args):
        heads = args[1].shape[1] // HD
        even = heads % 4 == 0 and mesh.shape["kv"] == 2 and mesh.shape["seq"] % 4 == 0
        return (paired_program if even else plain_program)(*args)

    return jax.shard_map(
        per_device,
        mesh=mesh,
        in_specs=placed,
        out_specs=(P(("seq", "kv"), None), P(("seq", "kv"), None)),
        check_vma=False,
    )
```

```python
import functools
import jax
import jax.numpy as jnp
from jax import lax
from jax.experimental import pallas as pl
from jax.experimental.pallas import tpu as pltpu
from jax.sharding import PartitionSpec as P

HD = 64
G = 8
WIN = 128
BACK = 8
LOG2E = 1.4426950408889634
SCORE_SCALE = HD ** (-0.5) * LOG2E
NEG = -1e30
SAFE_TOTAL = 2.0**100
NEVER = 2**30
FEATURES = 128
SHARD_LANE = 64
CUT = 2.0**15
TALL = HD + 16
PARAMS = pltpu.CompilerParams(
    dimension_semantics=("arbitrary",), vmem_limit_bytes=48 * 1024 * 1024
)


def interval_rows(starts_ref):
    lane = lax.broadcasted_iota(jnp.int32, (8, FEATURES), 1)
    begin = jnp.full((8, FEATURES), NEVER, jnp.int32)
    end = begin
    for i in range(starts_ref.shape[0]):
        entry = starts_ref[i]
        begin = jnp.where(lane == i, entry, begin)
        end = jnp.where(lane == i - 1, entry, end)
    return begin, end


def key_features(starts_ref, low, shard, rows):
    begin, end = interval_rows(starts_ref)
    u = low + lax.broadcasted_iota(jnp.int32, (rows, FEATURES), 0)
    lane = lax.broadcasted_iota(jnp.int32, (rows, FEATURES), 1)
    own = jnp.where(shard < 0, SHARD_LANE - 1, SHARD_LANE + shard)
    marked = (lane == own) | ((u >= begin[:1]) & (u < end[:1]))
    return jnp.where(marked, 1.0, 0.0).astype(jnp.bfloat16)


def query_features(starts_ref, low, named, rows):
    begin, end = (x.T[:, :1] for x in interval_rows(starts_ref))
    t = low + lax.broadcasted_iota(jnp.int32, (FEATURES, rows), 1)
    row = lax.broadcasted_iota(jnp.int32, (FEATURES, rows), 0)
    seen = (t >= begin) & (t < end) & (row < SHARD_LANE)
    for shard in named:
        seen = seen | ((row == SHARD_LANE + shard) & (shard >= 0))
    return jnp.where(seen, 0.0, -CUT).astype(jnp.bfloat16)


def score(key_block, query_cols):
    return jnp.dot(key_block, query_cols, preferred_element_type=jnp.float32) * SCORE_SCALE


def plain_weights(key_block, query_cols, bias=None):
    scores = score(key_block, query_cols)
    if bias is not None:
        scores = scores + bias
    return jnp.exp2(scores).astype(jnp.bfloat16)


def weigh(value_rows, weight):
    return jnp.dot(value_rows, weight, preferred_element_type=jnp.float32)


def topped(state, key_block, query_cols, value_rows, bias=None):
    top, acc = state
    scores = score(key_block, query_cols)
    if bias is not None:
        scores = scores + bias
    new_top = jnp.maximum(top, jnp.max(scores, axis=0, keepdims=True))
    weight = jnp.exp2(scores - new_top).astype(jnp.bfloat16)
    return new_top, acc * jnp.exp2(top - new_top) + weigh(value_rows, weight)


def fresh(total):
    row = lax.broadcasted_iota(jnp.int32, (TALL, total.shape[1]), 0)
    return jnp.where(row == HD, total, 0.0)


def slotted(col, head, heads):
    if heads == 1:
        return col
    empty = jnp.zeros_like(col)
    return jnp.concatenate([jnp.where(head == i, col, empty) for i in range(heads)], axis=0)


def overflowed(total):
    return jnp.max(jnp.where(total <= SAFE_TOTAL, 0.0, 1.0)) > 0.5


def sink_lanes(sink_ref, first, count, rows):
    return jnp.concatenate(
        [jnp.full((1, rows), sink_ref[first + e] * LOG2E, jnp.float32) for e in range(count)], axis=1
    )


class DocPlan:
    def __init__(self, first, last, grp, heads, earlier, units, rows, pieces, wide=8):
        self.first, self.last, self.grp, self.heads = first, last, grp, heads
        self.earlier, self.units, self.rows, self.pieces = earlier, units, rows, pieces
        self.wide = wide


def doc_body(plan, *refs):
    first, last, grp, heads, rows = plan.first, plan.last, plan.grp, plan.heads, plan.rows
    wide = plan.wide
    count = plan.earlier + plan.units
    refs = list(refs)
    where_ref, starts_ref, sink_ref = refs[:3]
    del refs[:3]
    list_refs = [refs.pop(0) for _ in range(grp)]
    query_refs = [refs.pop(0) for _ in range(grp)]
    unit_refs = [refs.pop(0) for _ in range(count)]
    if not first:
        acc_in = refs.pop(0)
    if last:
        piece_refs = [refs.pop(0) for _ in range(2 * grp if plan.pieces else 1)]
    else:
        acc_out = refs.pop(0)
    value_ref, key_ref, bias_ref, acc_ref, cols_ref = refs
    step = pl.program_id(0)
    core = where_ref[1]
    lowest = where_ref[0] - core
    width = heads * HD
    part = wide * rows
    lanes = grp * part
    new = range(plan.earlier, count)
    own = 0 if first or plan.earlier else -1

    def set_unit(n):
        unit = unit_refs[n][...]
        turned = unit[:, width:].T if width % 128 == 0 else unit.T[width:]
        for i in range(heads):
            value_ref[n, i, :HD] = turned[i * HD : (i + 1) * HD]
            value_ref[n, i, HD:] = jnp.ones((TALL - HD, grp * rows), jnp.bfloat16)
        key_ref[n, :, FEATURES:] = unit[:, :width]
        for r in range(grp):
            shard = lowest + (r ^ core) - where_ref[4 + n] if grp > 1 else lowest - where_ref[4 + n]
            marks = key_features(starts_ref, shard * rows, shard, rows)
            key_ref[n, r * rows : (r + 1) * rows, :FEATURES] = marks

    @pl.when(step == 0)
    def _():
        for n in new:
            set_unit(n)
        for a in range(grp):
            entries = [list_refs[0][0, i] for i in range(BACK)]
            if grp == 2:
                entries = [jnp.where(core == a, x, list_refs[1][0, i]) for i, x in enumerate(entries)]
            named = [lowest + a] + entries
            marks = query_features(starts_ref, (lowest + a) * rows, named, rows)
            for e in range(wide):
                spot = slice(a * part + e * rows, a * part + (e + 1) * rows)
                cols_ref[:FEATURES, spot] = marks
        if own == 0:
            u = lax.broadcasted_iota(jnp.int32, (rows, part), 0)
            t = jnp.bitwise_and(lax.broadcasted_iota(jnp.int32, (rows, part), 1), rows - 1)
            bias_ref[...] = jnp.where(u <= t, 0.0, NEG)

    head = step // (G // wide)
    sinks = sink_lanes(sink_ref, core * heads * G + wide * step, wide, rows)
    sinks = jnp.concatenate([sinks] * grp, axis=1)
    for a in range(grp):
        query = query_refs[0][...]
        if grp == 2:
            query = jnp.where(core == a, query, query_refs[1][...])
        turned = query.T
        for e in range(wide):
            spot = slice(a * part + e * rows, a * part + (e + 1) * rows)
            cols_ref[FEATURES:, spot] = slotted(turned[e * HD : (e + 1) * HD], head, heads)

    def own_span(r):
        return slice(0, rows) if grp == 1 else pl.ds(pl.multiple_of((r ^ core) * rows, rows), rows)

    def own_pairs():
        pairs = [(r, slice(r * part, (r + 1) * part), bias_ref[...]) for r in range(grp)]
        return pairs + ([(0, slice(part, lanes), None)] if grp == 2 else [])

    def rows_of(n):
        return [slice(r * rows, (r + 1) * rows) for r in range(grp)]

    gain = fresh(jnp.exp2(sinks)) if first else acc_in[0]
    gains = [gain[:, a * part : (a + 1) * part] for a in range(grp)]
    for n in new:
        if n == own:
            for r, span, bias in own_pairs():
                weight = plain_weights(key_ref[n, own_span(r)], cols_ref[:, span], bias)
                a = span.start // part
                gains[a] = gains[a] + weigh(value_ref[n, head, :, own_span(r)], weight)
            continue
        for a in range(grp):
            cols = cols_ref[:, a * part : (a + 1) * part]
            weights = [plain_weights(key_ref[n, span], cols) for span in rows_of(n)]
            gains[a] = gains[a] + weigh(value_ref[n, head], jnp.concatenate(weights, axis=0))
    for a in range(grp):
        acc_ref[:, a * part : (a + 1) * part] = gains[a]

    if not last:
        acc_out[0] = acc_ref[...]
        return

    @pl.when(overflowed(acc_ref[HD : HD + 1]))
    def _():
        for n in range(plan.earlier):
            set_unit(n)
        for a in range(grp):
            spot = slice(a * part, (a + 1) * part)
            state = sinks[:, spot], fresh(jnp.ones((1, part), jnp.float32))
            for r, span, bias in own_pairs():
                if span.start == a * part:
                    values = value_ref[0, head, :, own_span(r)]
                    state = topped(state, key_ref[0, own_span(r)], cols_ref[:, spot], values, bias)
            for n in range(1, count):
                for span in rows_of(n):
                    values = value_ref[n, head, :, span]
                    state = topped(state, key_ref[n, span], cols_ref[:, spot], values)
            acc_ref[:, spot] = state[1]

    result = acc_ref[:HD] * (1.0 / acc_ref[HD : HD + 1])
    blocks = []
    for a in range(grp):
        parts = [result[:, a * part + e * rows : a * part + (e + 1) * rows] for e in range(wide)]
        blocks.append(jnp.concatenate(parts, axis=0).T.astype(jnp.bfloat16))
    if not plan.pieces:
        piece_refs[0][...] = blocks[0]
        return
    half = rows // 2
    side = where_ref[2]
    for a in range(grp):
        block = jnp.where(core == a, blocks[0], blocks[1])
        low, high = block[:half], block[half:]
        piece_refs[2 * a][...] = jnp.where(side == 0, low, high)
        piece_refs[2 * a + 1][...] = jnp.where(side == 0, high, low)


def doc_call(plan, where, starts, sinks, lists, queries, units, state, columns):
    grp, heads, rows, wide = plan.grp, plan.heads, plan.rows, plan.wide
    steps = heads * G // wide
    size = wide * HD
    width = heads * HD
    count = plan.earlier + plan.units
    smem = pl.BlockSpec(memory_space=pltpu.SMEM)
    args = [where, starts, sinks, *lists]
    specs = [smem] * (2 + grp)
    args += list(queries)
    specs.append(pl.BlockSpec((rows, size), lambda j, w: (0, w[1] * steps + j)))
    if grp == 2:
        specs.append(pl.BlockSpec((rows, size), lambda j, w: (0, j)))
    for unit in units:
        args.append(unit)
        specs.append(pl.BlockSpec((grp * rows, 2 * width), lambda j, w: (0, 0)))
    lanes = wide * grp * rows
    state_spec = pl.BlockSpec((1, TALL, lanes), lambda j, w: (j, 0, 0))
    aliases = {}
    if not plan.first:
        if not plan.last:
            aliases = {len(args): 0}
        args.append(state)
        specs.append(state_spec)
    if not plan.last:
        out_shape = [jax.ShapeDtypeStruct((steps, TALL, lanes), jnp.float32)]
        out_specs = [state_spec]
    elif plan.pieces:
        half = rows // 2
        out_shape = [jax.ShapeDtypeStruct((half, columns), jnp.bfloat16)]
        out_specs = [pl.BlockSpec((half, size), lambda j, w: (0, w[3] * steps + j))]
        for _ in range(2 * grp - 1):
            out_shape.append(jax.ShapeDtypeStruct((half, steps * size), jnp.bfloat16))
            out_specs.append(pl.BlockSpec((half, size), lambda j, w: (0, j)))
    else:
        out_shape = [jax.ShapeDtypeStruct((rows, steps * size), jnp.bfloat16)]
        out_specs = [pl.BlockSpec((rows, size), lambda j, w: (0, j))]
    return pl.pallas_call(
        functools.partial(doc_body, plan),
        out_shape=out_shape,
        grid_spec=pltpu.PrefetchScalarGridSpec(
            num_scalar_prefetch=1,
            grid=(steps,),
            in_specs=specs,
            out_specs=out_specs,
            scratch_shapes=[
                pltpu.VMEM((count, heads, TALL, grp * rows), jnp.bfloat16),
                pltpu.VMEM((count, grp * rows, FEATURES + width), jnp.bfloat16),
                pltpu.VMEM((rows, wide * rows), jnp.float32),
                pltpu.VMEM((TALL, lanes), jnp.float32),
                pltpu.VMEM((FEATURES + width, lanes), jnp.bfloat16),
            ],
        ),
        input_output_aliases=aliases,
        compiler_params=PARAMS,
        name="doc_attention",
    )(*args)


def band_body(heads, rows, wide, pieces, where_ref, starts_ref, sink_ref, query_ref, key_ref, value_ref, rim_ref, *refs):
    out_refs, (keys, values, bias_ref, cols_ref, acc_ref) = refs[:-5], refs[-5:]
    step = pl.program_id(0)
    width = heads * HD
    low = where_ref[0] * rows
    tiles = rows // WIN
    lanes = wide * WIN

    @pl.when(step == 0)
    def _():
        rim = rim_ref[...]
        keys[:WIN, FEATURES:] = rim[:, :width]
        keys[WIN:, FEATURES:] = key_ref[...]
        shard = where_ref[0]
        keys[:WIN, :FEATURES] = key_features(starts_ref, low - WIN, shard - 1, WIN)
        keys[WIN:, :FEATURES] = key_features(starts_ref, low, shard, rows)
        turned_rim = rim[:, width:].T if width % 128 == 0 else rim.T[width:]
        turned_own = value_ref[...].T
        for i in range(heads):
            values[i, :HD, :WIN] = turned_rim[i * HD : (i + 1) * HD]
            values[i, :HD, WIN:] = turned_own[i * HD : (i + 1) * HD]
            values[i, HD:] = jnp.ones((TALL - HD, rows + WIN), jnp.bfloat16)
        marks = query_features(starts_ref, low, [shard, shard - 1], rows)
        for tile in range(tiles):
            for e in range(wide):
                cols_ref[tile, :FEATURES, e * WIN : (e + 1) * WIN] = marks[:, tile * WIN : (tile + 1) * WIN]
        u = lax.broadcasted_iota(jnp.int32, (2 * WIN, lanes), 0)
        t = jnp.bitwise_and(lax.broadcasted_iota(jnp.int32, (2 * WIN, lanes), 1), WIN - 1)
        bias_ref[...] = jnp.where((u <= t + WIN) & (u > t), 0.0, NEG)

    head = step // (G // wide)
    turned = query_ref[...].T
    sinks = sink_lanes(sink_ref, wide * step, wide, WIN)

    for tile in range(tiles):
        span = slice(tile * WIN, (tile + 1) * WIN)
        for e in range(wide):
            col = slotted(turned[e * HD : (e + 1) * HD, span], head, heads)
            cols_ref[tile, FEATURES:, e * WIN : (e + 1) * WIN] = col
    for tile in range(tiles):
        span = slice(tile * WIN, (tile + 2) * WIN)
        weight = plain_weights(keys[span], cols_ref[tile], bias_ref[...])
        acc_ref[tile] = fresh(jnp.exp2(sinks)) + weigh(values[head, :, span], weight)

    @pl.when(overflowed(acc_ref[:, HD : HD + 1]))
    def _():
        for tile in range(tiles):
            span = slice(tile * WIN, (tile + 2) * WIN)
            state = sinks, fresh(jnp.ones((1, lanes), jnp.float32))
            state = topped(state, keys[span], cols_ref[tile], values[head, :, span], bias_ref[...])
            acc_ref[tile] = state[1]

    finished = []
    for tile in range(tiles):
        result = acc_ref[tile, :HD] * (1.0 / acc_ref[tile, HD : HD + 1])
        parts = [result[:, e * WIN : (e + 1) * WIN] for e in range(wide)]
        finished.append(jnp.concatenate(parts, axis=0).T.astype(jnp.bfloat16))
    if pieces:
        side = where_ref[2]
        out_refs[0][...] = jnp.where(side == 0, finished[0], finished[1])
        out_refs[1][...] = jnp.where(side == 0, finished[1], finished[0])
    else:
        for tile, value in enumerate(finished):
            out_refs[0][tile * WIN : (tile + 1) * WIN] = value


def band_call(where, starts, sinks, queries, keys, value_rows, rim, heads, rows, pieces, columns):
    wide = 8
    steps = heads * G // wide
    size = wide * HD
    width = heads * HD
    tiles = rows // WIN
    smem = pl.BlockSpec(memory_space=pltpu.SMEM)
    if pieces:
        out_shape = [
            jax.ShapeDtypeStruct((WIN, columns), jnp.bfloat16),
            jax.ShapeDtypeStruct((WIN, steps * size), jnp.bfloat16),
        ]
        out_specs = [
            pl.BlockSpec((WIN, size), lambda j, w: (0, w[2] * steps + j)),
            pl.BlockSpec((WIN, size), lambda j, w: (0, j)),
        ]
    else:
        out_shape = [jax.ShapeDtypeStruct((rows, steps * size), jnp.bfloat16)]
        out_specs = [pl.BlockSpec((rows, size), lambda j, w: (0, j))]

    def fixed(j, w):
        return (0, 0)

    return pl.pallas_call(
        functools.partial(band_body, heads, rows, wide, pieces),
        out_shape=out_shape,
        grid_spec=pltpu.PrefetchScalarGridSpec(
            num_scalar_prefetch=1,
            grid=(steps,),
            in_specs=[
                smem,
                smem,
                pl.BlockSpec((rows, size), lambda j, w: (0, j)),
                pl.BlockSpec((rows, width), fixed),
                pl.BlockSpec((rows, width), fixed),
                pl.BlockSpec((WIN, 2 * width), fixed),
            ],
            out_specs=out_specs,
            scratch_shapes=[
                pltpu.VMEM((rows + WIN, FEATURES + width), jnp.bfloat16),
                pltpu.VMEM((heads, TALL, rows + WIN), jnp.bfloat16),
                pltpu.VMEM((2 * WIN, wide * WIN), jnp.float32),
                pltpu.VMEM((tiles, FEATURES + width, wide * WIN), jnp.bfloat16),
                pltpu.VMEM((tiles, TALL, wide * WIN), jnp.float32),
            ],
        ),
        compiler_params=PARAMS,
        name="band_attention",
    )(where, starts, sinks, queries, keys, value_rows, rim)


def shifted(value, steps):
    count = lax.axis_size("seq")
    return lax.ppermute(value, "seq", [(i, i + steps) for i in range(count - steps)])


def swapped(value, bit):
    count = lax.axis_size("seq")
    return lax.ppermute(value, "seq", [(i, i ^ bit) for i in range(count)])


def relay(result):
    return lax.all_to_all(result, "kv", split_axis=0, concat_axis=1, tiled=True)


def paired_program(
    q_band, k_band, v_band, sink_band, q_doc, k_doc, v_doc, sink_doc, doc_starts, source_lists
):
    rows = q_band.shape[0]
    heads = k_band.shape[1] // HD
    mine = heads // 2
    width = mine * HD
    columns = 2 * q_band.shape[1]
    shard, side = lax.axis_index("seq"), lax.axis_index("kv")
    core = shard % 2
    layer = shard // 2 % 2
    flip = 4 * layer - 2

    def place(*dists):
        return jnp.stack([shard, core, side, 2 * side + core, *dists]).astype(jnp.int32)

    def half(value, which, size):
        return lax.dynamic_slice_in_dim(value, which * size, size, axis=1)

    away = jnp.concatenate([half(k_doc, 1 - core, width), half(v_doc, 1 - core, width)], axis=1)
    away, mate_lists = lax.optimization_barrier((away, swapped(source_lists, 1)))
    near = swapped(away, 1)
    rim = jnp.concatenate([k_band[rows - WIN :], v_band[rows - WIN :]], axis=1)
    rim_sent, rim = rim, shifted(rim, 1)
    kept = jnp.concatenate([half(k_doc, core, width), half(v_doc, core, width)], axis=1)
    unit = jnp.concatenate([kept, near], axis=0)
    back4 = shifted(unit, 4)
    back8 = shifted(unit, 8)
    q_later, _, _ = lax.optimization_barrier((q_doc, unit, rim_sent))
    q_mate = swapped(half(q_later, 1 - core, mine * G * HD), 1)
    cross4 = swapped(back4, 2)
    band_out, band_send = band_call(
        place(), doc_starts, sink_band, q_band, k_band, v_band, rim, heads, rows, True, columns
    )
    band_got = lax.ppermute(band_send, "kv", [(0, 1), (1, 0)])
    out_band = lax.dynamic_update_slice(band_out, band_got, (0, (1 - side) * q_band.shape[1]))

    def doc(first, last, units, dists, earlier, state):
        plan = DocPlan(first, last, 2, mine, earlier, len(units) - earlier, rows, True)
        return doc_call(
            plan, place(*dists), doc_starts, sink_doc, (source_lists, mate_lists),
            (q_doc, q_mate), units, state, columns,
        )

    dists = [0, 4, 4 + flip, 8, jnp.where(layer == 0, 6, 2)]
    units = [unit, back4]
    (state,) = doc(True, False, units, dists[:2], 0, None)
    state, back8 = lax.optimization_barrier((state, back8))
    late = swapped(jnp.where(layer == 0, unit, back8), 2)
    units += [cross4, back8, late]
    (state,) = doc(False, False, units[2:4], dists[2:4], 0, state)
    out_doc, *sends = doc(False, True, units, dists, 4, state)
    size = mine * G * HD
    for mask, send in zip((1, 2, 3), sends):
        count = 2 * lax.axis_size("seq")
        got = lax.ppermute(send, ("seq", "kv"), [(i, i ^ mask) for i in range(count)])
        source = ((2 * side + core) ^ (mask & 1) * 2 ^ (mask >> 1)) * size
        out_doc = lax.dynamic_update_slice(out_doc, got, (0, source))
    return out_band, out_doc


def plain_program(
    q_band, k_band, v_band, sink_band, q_doc, k_doc, v_doc, sink_doc, doc_starts, source_lists
):
    rows = q_band.shape[0]
    heads = k_band.shape[1] // HD
    shard = lax.axis_index("seq")

    def place(*dists):
        return jnp.stack([shard, 0, 0, 0, *dists]).astype(jnp.int32)

    rim = jnp.concatenate([k_band[rows - WIN :], v_band[rows - WIN :]], axis=1)
    rim = shifted(rim, 1)
    unit = jnp.concatenate([k_doc, v_doc], axis=1)
    units = [unit] + [shifted(unit, d) for d in range(1, BACK + 1)]
    band = band_call(
        place(), doc_starts, sink_band, q_band, k_band, v_band, rim, heads, rows, False, None
    )[0]
    plan = DocPlan(True, True, 1, heads, 0, BACK + 1, rows, False)
    doc = doc_call(
        plan, place(*range(BACK + 1)), doc_starts, sink_doc, (source_lists,),
        (q_doc,), units, None, None,
    )[0]
    return relay(band), relay(doc)


def solution(mesh):
    placed = (
        P("seq", "kv"),
        P("seq", "kv"),
        P("seq", "kv"),
        P("kv"),
        P("seq", "kv"),
        P("seq", "kv"),
        P("seq", "kv"),
        P("kv"),
        P(),
        P("seq", None),
    )

    def per_device(*args):
        heads = args[1].shape[1] // HD
        even = heads % 4 == 0 and mesh.shape["kv"] == 2 and mesh.shape["seq"] % 4 == 0
        return (paired_program if even else plain_program)(*args)

    return jax.shard_map(
        per_device,
        mesh=mesh,
        in_specs=placed,
        out_specs=(P(("seq", "kv"), None), P(("seq", "kv"), None)),
        check_vma=False,
    )
```

```python
import functools
import jax
import jax.numpy as jnp
from jax import lax
from jax.experimental import pallas as pl
from jax.experimental.pallas import tpu as pltpu
from jax.sharding import PartitionSpec as P

HD = 64
G = 8
WIN = 128
BACK = 8
LOG2E = 1.4426950408889634
SCORE_SCALE = HD ** (-0.5) * LOG2E
NEG = -1e30
SAFE_TOTAL = 2.0**100
NEVER = 2**30
FEATURES = 128
SHARD_LANE = 64
CUT = 2.0**15
TALL = HD + 16
PARAMS = pltpu.CompilerParams(
    dimension_semantics=("arbitrary",), vmem_limit_bytes=48 * 1024 * 1024
)


def interval_rows(starts_ref):
    lane = lax.broadcasted_iota(jnp.int32, (8, FEATURES), 1)
    begin = jnp.full((8, FEATURES), NEVER, jnp.int32)
    end = begin
    for i in range(starts_ref.shape[0]):
        entry = starts_ref[i]
        begin = jnp.where(lane == i, entry, begin)
        end = jnp.where(lane == i - 1, entry, end)
    return begin, end


def key_features(starts_ref, low, shard, rows):
    begin, end = interval_rows(starts_ref)
    u = low + lax.broadcasted_iota(jnp.int32, (rows, FEATURES), 0)
    lane = lax.broadcasted_iota(jnp.int32, (rows, FEATURES), 1)
    own = jnp.where(shard < 0, SHARD_LANE - 1, SHARD_LANE + shard)
    marked = (lane == own) | ((u >= begin[:1]) & (u < end[:1]))
    return jnp.where(marked, 1.0, 0.0).astype(jnp.bfloat16)


def query_features(starts_ref, low, named, rows):
    begin, end = (x.T[:, :1] for x in interval_rows(starts_ref))
    t = low + lax.broadcasted_iota(jnp.int32, (FEATURES, rows), 1)
    row = lax.broadcasted_iota(jnp.int32, (FEATURES, rows), 0)
    seen = (t >= begin) & (t < end) & (row < SHARD_LANE)
    for shard in named:
        seen = seen | ((row == SHARD_LANE + shard) & (shard >= 0))
    return jnp.where(seen, 0.0, -CUT).astype(jnp.bfloat16)


def score(key_block, query_cols):
    return jnp.dot(key_block, query_cols, preferred_element_type=jnp.float32) * SCORE_SCALE


def plain_weights(key_block, query_cols, bias=None):
    scores = score(key_block, query_cols)
    if bias is not None:
        scores = scores + bias
    return jnp.exp2(scores).astype(jnp.bfloat16)


def weigh(value_rows, weight):
    return jnp.dot(value_rows, weight, preferred_element_type=jnp.float32)


def topped(state, key_block, query_cols, value_rows, bias=None):
    top, acc = state
    scores = score(key_block, query_cols)
    if bias is not None:
        scores = scores + bias
    new_top = jnp.maximum(top, jnp.max(scores, axis=0, keepdims=True))
    weight = jnp.exp2(scores - new_top).astype(jnp.bfloat16)
    return new_top, acc * jnp.exp2(top - new_top) + weigh(value_rows, weight)


def fresh(total):
    row = lax.broadcasted_iota(jnp.int32, (TALL, total.shape[1]), 0)
    return jnp.where(row == HD, total, 0.0)


def slotted(col, head, heads):
    if heads == 1:
        return col
    empty = jnp.zeros_like(col)
    return jnp.concatenate([jnp.where(head == i, col, empty) for i in range(heads)], axis=0)


def overflowed(total):
    return jnp.max(jnp.where(total <= SAFE_TOTAL, 0.0, 1.0)) > 0.5


def sink_lanes(sink_ref, first, count, rows):
    return jnp.concatenate(
        [jnp.full((1, rows), sink_ref[first + e] * LOG2E, jnp.float32) for e in range(count)], axis=1
    )


class DocPlan:
    def __init__(self, first, last, grp, heads, earlier, units, rows, pieces, wide=8):
        self.first, self.last, self.grp, self.heads = first, last, grp, heads
        self.earlier, self.units, self.rows, self.pieces = earlier, units, rows, pieces
        self.wide = wide


def doc_body(plan, *refs):
    first, last, grp, heads, rows = plan.first, plan.last, plan.grp, plan.heads, plan.rows
    wide = plan.wide
    count = plan.earlier + plan.units
    refs = list(refs)
    where_ref, starts_ref, sink_ref = refs[:3]
    del refs[:3]
    list_refs = [refs.pop(0) for _ in range(grp)]
    query_refs = [refs.pop(0) for _ in range(grp)]
    unit_refs = [refs.pop(0) for _ in range(count)]
    if not first:
        acc_in = refs.pop(0)
    if last:
        piece_refs = [refs.pop(0) for _ in range(2 * grp if plan.pieces else 1)]
    else:
        acc_out = refs.pop(0)
    value_ref, key_ref, bias_ref, acc_ref, cols_ref = refs
    step = pl.program_id(0)
    core = where_ref[1]
    lowest = where_ref[0] - core
    width = heads * HD
    part = wide * rows
    lanes = grp * part
    new = range(plan.earlier, count)
    own = 0 if first or plan.earlier else -1

    def set_unit(n):
        unit = unit_refs[n][...]
        turned = unit[:, width:].T if width % 128 == 0 else unit.T[width:]
        for i in range(heads):
            value_ref[n, i, :HD] = turned[i * HD : (i + 1) * HD]
            value_ref[n, i, HD:] = jnp.ones((TALL - HD, grp * rows), jnp.bfloat16)
        key_ref[n, :, FEATURES:] = unit[:, :width]
        for r in range(grp):
            shard = lowest + (r ^ core) - where_ref[4 + n] if grp > 1 else lowest - where_ref[4 + n]
            marks = key_features(starts_ref, shard * rows, shard, rows)
            key_ref[n, r * rows : (r + 1) * rows, :FEATURES] = marks

    @pl.when(step == 0)
    def _():
        for n in new:
            set_unit(n)
        for a in range(grp):
            entries = [list_refs[0][0, i] for i in range(BACK)]
            if grp == 2:
                entries = [jnp.where(core == a, x, list_refs[1][0, i]) for i, x in enumerate(entries)]
            named = [lowest + a] + entries
            marks = query_features(starts_ref, (lowest + a) * rows, named, rows)
            for e in range(wide):
                spot = slice(a * part + e * rows, a * part + (e + 1) * rows)
                cols_ref[:FEATURES, spot] = marks
        if own == 0:
            u = lax.broadcasted_iota(jnp.int32, (rows, part), 0)
            t = jnp.bitwise_and(lax.broadcasted_iota(jnp.int32, (rows, part), 1), rows - 1)
            bias_ref[...] = jnp.where(u <= t, 0.0, NEG)

    head = step // (G // wide)
    sinks = sink_lanes(sink_ref, core * heads * G + wide * step, wide, rows)
    sinks = jnp.concatenate([sinks] * grp, axis=1)
    for a in range(grp):
        query = query_refs[0][...]
        if grp == 2:
            query = jnp.where(core == a, query, query_refs[1][...])
        turned = query.T
        for e in range(wide):
            spot = slice(a * part + e * rows, a * part + (e + 1) * rows)
            cols_ref[FEATURES:, spot] = slotted(turned[e * HD : (e + 1) * HD], head, heads)

    def own_span(r):
        return slice(0, rows) if grp == 1 else pl.ds(pl.multiple_of((r ^ core) * rows, rows), rows)

    def own_pairs():
        pairs = [(r, slice(r * part, (r + 1) * part), bias_ref[...]) for r in range(grp)]
        return pairs + ([(0, slice(part, lanes), None)] if grp == 2 else [])

    def rows_of(n):
        return [slice(r * rows, (r + 1) * rows) for r in range(grp)]

    gain = fresh(jnp.exp2(sinks)) if first else acc_in[0]
    gains = [gain[:, a * part : (a + 1) * part] for a in range(grp)]
    for n in new:
        if n == own:
            for r, span, bias in own_pairs():
                weight = plain_weights(key_ref[n, own_span(r)], cols_ref[:, span], bias)
                a = span.start // part
                gains[a] = gains[a] + weigh(value_ref[n, head, :, own_span(r)], weight)
            continue
        for a in range(grp):
            cols = cols_ref[:, a * part : (a + 1) * part]
            weights = [plain_weights(key_ref[n, span], cols) for span in rows_of(n)]
            gains[a] = gains[a] + weigh(value_ref[n, head], jnp.concatenate(weights, axis=0))
    for a in range(grp):
        acc_ref[:, a * part : (a + 1) * part] = gains[a]

    if not last:
        acc_out[0] = acc_ref[...]
        return

    @pl.when(overflowed(acc_ref[HD : HD + 1]))
    def _():
        for n in range(plan.earlier):
            set_unit(n)
        for a in range(grp):
            spot = slice(a * part, (a + 1) * part)
            state = sinks[:, spot], fresh(jnp.ones((1, part), jnp.float32))
            for r, span, bias in own_pairs():
                if span.start == a * part:
                    values = value_ref[0, head, :, own_span(r)]
                    state = topped(state, key_ref[0, own_span(r)], cols_ref[:, spot], values, bias)
            for n in range(1, count):
                for span in rows_of(n):
                    values = value_ref[n, head, :, span]
                    state = topped(state, key_ref[n, span], cols_ref[:, spot], values)
            acc_ref[:, spot] = state[1]

    result = acc_ref[:HD] * (1.0 / acc_ref[HD : HD + 1])
    blocks = []
    for a in range(grp):
        parts = [result[:, a * part + e * rows : a * part + (e + 1) * rows] for e in range(wide)]
        blocks.append(jnp.concatenate(parts, axis=0).T.astype(jnp.bfloat16))
    if not plan.pieces:
        piece_refs[0][...] = blocks[0]
        return
    half = rows // 2
    side = where_ref[2]
    for a in range(grp):
        block = jnp.where(core == a, blocks[0], blocks[1])
        low, high = block[:half], block[half:]
        piece_refs[2 * a][...] = jnp.where(side == 0, low, high)
        piece_refs[2 * a + 1][...] = jnp.where(side == 0, high, low)


def doc_call(plan, where, starts, sinks, lists, queries, units, state, columns):
    grp, heads, rows, wide = plan.grp, plan.heads, plan.rows, plan.wide
    steps = heads * G // wide
    size = wide * HD
    width = heads * HD
    count = plan.earlier + plan.units
    smem = pl.BlockSpec(memory_space=pltpu.SMEM)
    args = [where, starts, sinks, *lists]
    specs = [smem] * (2 + grp)
    args += list(queries)
    specs.append(pl.BlockSpec((rows, size), lambda j, w: (0, w[1] * steps + j)))
    if grp == 2:
        specs.append(pl.BlockSpec((rows, size), lambda j, w: (0, j)))
    for unit in units:
        args.append(unit)
        specs.append(pl.BlockSpec((grp * rows, 2 * width), lambda j, w: (0, 0)))
    lanes = wide * grp * rows
    state_spec = pl.BlockSpec((1, TALL, lanes), lambda j, w: (j, 0, 0))
    aliases = {}
    if not plan.first:
        if not plan.last:
            aliases = {len(args): 0}
        args.append(state)
        specs.append(state_spec)
    if not plan.last:
        out_shape = [jax.ShapeDtypeStruct((steps, TALL, lanes), jnp.float32)]
        out_specs = [state_spec]
    elif plan.pieces:
        half = rows // 2
        out_shape = [jax.ShapeDtypeStruct((half, columns), jnp.bfloat16)]
        out_specs = [pl.BlockSpec((half, size), lambda j, w: (0, w[3] * steps + j))]
        for _ in range(2 * grp - 1):
            out_shape.append(jax.ShapeDtypeStruct((half, steps * size), jnp.bfloat16))
            out_specs.append(pl.BlockSpec((half, size), lambda j, w: (0, j)))
    else:
        out_shape = [jax.ShapeDtypeStruct((rows, steps * size), jnp.bfloat16)]
        out_specs = [pl.BlockSpec((rows, size), lambda j, w: (0, j))]
    return pl.pallas_call(
        functools.partial(doc_body, plan),
        out_shape=out_shape,
        grid_spec=pltpu.PrefetchScalarGridSpec(
            num_scalar_prefetch=1,
            grid=(steps,),
            in_specs=specs,
            out_specs=out_specs,
            scratch_shapes=[
                pltpu.VMEM((count, heads, TALL, grp * rows), jnp.bfloat16),
                pltpu.VMEM((count, grp * rows, FEATURES + width), jnp.bfloat16),
                pltpu.VMEM((rows, wide * rows), jnp.float32),
                pltpu.VMEM((TALL, lanes), jnp.float32),
                pltpu.VMEM((FEATURES + width, lanes), jnp.bfloat16),
            ],
        ),
        input_output_aliases=aliases,
        compiler_params=PARAMS,
        name="doc_attention",
    )(*args)


def band_body(heads, rows, wide, pieces, where_ref, starts_ref, sink_ref, query_ref, key_ref, value_ref, rim_ref, *refs):
    out_refs, (keys, values, bias_ref, cols_ref, acc_ref) = refs[:-5], refs[-5:]
    step = pl.program_id(0)
    width = heads * HD
    low = where_ref[0] * rows
    tiles = rows // WIN
    lanes = wide * WIN

    @pl.when(step == 0)
    def _():
        rim = rim_ref[...]
        keys[:WIN, FEATURES:] = rim[:, :width]
        keys[WIN:, FEATURES:] = key_ref[...]
        shard = where_ref[0]
        keys[:WIN, :FEATURES] = key_features(starts_ref, low - WIN, shard - 1, WIN)
        keys[WIN:, :FEATURES] = key_features(starts_ref, low, shard, rows)
        turned_rim = rim[:, width:].T if width % 128 == 0 else rim.T[width:]
        turned_own = value_ref[...].T
        for i in range(heads):
            values[i, :HD, :WIN] = turned_rim[i * HD : (i + 1) * HD]
            values[i, :HD, WIN:] = turned_own[i * HD : (i + 1) * HD]
            values[i, HD:] = jnp.ones((TALL - HD, rows + WIN), jnp.bfloat16)
        marks = query_features(starts_ref, low, [shard, shard - 1], rows)
        for tile in range(tiles):
            for e in range(wide):
                cols_ref[tile, :FEATURES, e * WIN : (e + 1) * WIN] = marks[:, tile * WIN : (tile + 1) * WIN]
        u = lax.broadcasted_iota(jnp.int32, (2 * WIN, lanes), 0)
        t = jnp.bitwise_and(lax.broadcasted_iota(jnp.int32, (2 * WIN, lanes), 1), WIN - 1)
        bias_ref[...] = jnp.where((u <= t + WIN) & (u > t), 0.0, NEG)

    head = step // (G // wide)
    turned = query_ref[...].T
    sinks = sink_lanes(sink_ref, wide * step, wide, WIN)

    for tile in range(tiles):
        span = slice(tile * WIN, (tile + 1) * WIN)
        for e in range(wide):
            col = slotted(turned[e * HD : (e + 1) * HD, span], head, heads)
            cols_ref[tile, FEATURES:, e * WIN : (e + 1) * WIN] = col
    for tile in range(tiles):
        span = slice(tile * WIN, (tile + 2) * WIN)
        weight = plain_weights(keys[span], cols_ref[tile], bias_ref[...])
        acc_ref[tile] = fresh(jnp.exp2(sinks)) + weigh(values[head, :, span], weight)

    @pl.when(overflowed(acc_ref[:, HD : HD + 1]))
    def _():
        for tile in range(tiles):
            span = slice(tile * WIN, (tile + 2) * WIN)
            state = sinks, fresh(jnp.ones((1, lanes), jnp.float32))
            state = topped(state, keys[span], cols_ref[tile], values[head, :, span], bias_ref[...])
            acc_ref[tile] = state[1]

    finished = []
    for tile in range(tiles):
        result = acc_ref[tile, :HD] * (1.0 / acc_ref[tile, HD : HD + 1])
        parts = [result[:, e * WIN : (e + 1) * WIN] for e in range(wide)]
        finished.append(jnp.concatenate(parts, axis=0).T.astype(jnp.bfloat16))
    if pieces:
        side = where_ref[2]
        out_refs[0][...] = jnp.where(side == 0, finished[0], finished[1])
        out_refs[1][...] = jnp.where(side == 0, finished[1], finished[0])
    else:
        for tile, value in enumerate(finished):
            out_refs[0][tile * WIN : (tile + 1) * WIN] = value


def band_call(where, starts, sinks, queries, keys, value_rows, rim, heads, rows, pieces, columns):
    wide = 8
    steps = heads * G // wide
    size = wide * HD
    width = heads * HD
    tiles = rows // WIN
    smem = pl.BlockSpec(memory_space=pltpu.SMEM)
    if pieces:
        out_shape = [
            jax.ShapeDtypeStruct((WIN, columns), jnp.bfloat16),
            jax.ShapeDtypeStruct((WIN, steps * size), jnp.bfloat16),
        ]
        out_specs = [
            pl.BlockSpec((WIN, size), lambda j, w: (0, w[2] * steps + j)),
            pl.BlockSpec((WIN, size), lambda j, w: (0, j)),
        ]
    else:
        out_shape = [jax.ShapeDtypeStruct((rows, steps * size), jnp.bfloat16)]
        out_specs = [pl.BlockSpec((rows, size), lambda j, w: (0, j))]

    def fixed(j, w):
        return (0, 0)

    return pl.pallas_call(
        functools.partial(band_body, heads, rows, wide, pieces),
        out_shape=out_shape,
        grid_spec=pltpu.PrefetchScalarGridSpec(
            num_scalar_prefetch=1,
            grid=(steps,),
            in_specs=[
                smem,
                smem,
                pl.BlockSpec((rows, size), lambda j, w: (0, j)),
                pl.BlockSpec((rows, width), fixed),
                pl.BlockSpec((rows, width), fixed),
                pl.BlockSpec((WIN, 2 * width), fixed),
            ],
            out_specs=out_specs,
            scratch_shapes=[
                pltpu.VMEM((rows + WIN, FEATURES + width), jnp.bfloat16),
                pltpu.VMEM((heads, TALL, rows + WIN), jnp.bfloat16),
                pltpu.VMEM((2 * WIN, wide * WIN), jnp.float32),
                pltpu.VMEM((tiles, FEATURES + width, wide * WIN), jnp.bfloat16),
                pltpu.VMEM((tiles, TALL, wide * WIN), jnp.float32),
            ],
        ),
        compiler_params=PARAMS,
        name="band_attention",
    )(where, starts, sinks, queries, keys, value_rows, rim)


def shifted(value, steps):
    count = lax.axis_size("seq")
    return lax.ppermute(value, "seq", [(i, i + steps) for i in range(count - steps)])


def swapped(value, bit):
    count = lax.axis_size("seq")
    return lax.ppermute(value, "seq", [(i, i ^ bit) for i in range(count)])


def relay(result):
    return lax.all_to_all(result, "kv", split_axis=0, concat_axis=1, tiled=True)


def paired_program(
    q_band, k_band, v_band, sink_band, q_doc, k_doc, v_doc, sink_doc, doc_starts, source_lists
):
    rows = q_band.shape[0]
    heads = k_band.shape[1] // HD
    mine = heads // 2
    width = mine * HD
    columns = 2 * q_band.shape[1]
    shard, side = lax.axis_index("seq"), lax.axis_index("kv")
    core = shard % 2
    layer = shard // 2 % 2
    flip = 4 * layer - 2

    def place(*dists):
        return jnp.stack([shard, core, side, 2 * side + core, *dists]).astype(jnp.int32)

    def half(value, which, size):
        return lax.dynamic_slice_in_dim(value, which * size, size, axis=1)

    away = jnp.concatenate([half(k_doc, 1 - core, width), half(v_doc, 1 - core, width)], axis=1)
    away, mate_lists = lax.optimization_barrier((away, swapped(source_lists, 1)))
    near = swapped(away, 1)
    rim = jnp.concatenate([k_band[rows - WIN :], v_band[rows - WIN :]], axis=1)
    rim = shifted(rim, 1)
    kept = jnp.concatenate([half(k_doc, core, width), half(v_doc, core, width)], axis=1)
    unit = jnp.concatenate([kept, near], axis=0)
    unit, rim = lax.optimization_barrier((unit, rim))
    back4 = shifted(unit, 4)
    back8 = shifted(unit, 8)
    q_later, _ = lax.optimization_barrier((q_doc, unit))
    q_mate = swapped(half(q_later, 1 - core, mine * G * HD), 1)
    cross4 = swapped(back4, 2)
    band_out, band_send = band_call(
        place(), doc_starts, sink_band, q_band, k_band, v_band, rim, heads, rows, True, columns
    )
    band_got = lax.ppermute(band_send, "kv", [(0, 1), (1, 0)])
    out_band = lax.dynamic_update_slice(band_out, band_got, (0, (1 - side) * q_band.shape[1]))

    def doc(first, last, units, dists, earlier, state):
        plan = DocPlan(first, last, 2, mine, earlier, len(units) - earlier, rows, True)
        return doc_call(
            plan, place(*dists), doc_starts, sink_doc, (source_lists, mate_lists),
            (q_doc, q_mate), units, state, columns,
        )

    dists = [0, 4, 4 + flip, 8, jnp.where(layer == 0, 6, 2)]
    units = [unit, back4]
    (state,) = doc(True, False, units, dists[:2], 0, None)
    state, back8 = lax.optimization_barrier((state, back8))
    late = swapped(jnp.where(layer == 0, unit, back8), 2)
    units += [cross4, back8, late]
    (state,) = doc(False, False, units[2:4], dists[2:4], 0, state)
    out_doc, *sends = doc(False, True, units, dists, 4, state)
    size = mine * G * HD
    for mask, send in zip((1, 2, 3), sends):
        count = 2 * lax.axis_size("seq")
        got = lax.ppermute(send, ("seq", "kv"), [(i, i ^ mask) for i in range(count)])
        source = ((2 * side + core) ^ (mask & 1) * 2 ^ (mask >> 1)) * size
        out_doc = lax.dynamic_update_slice(out_doc, got, (0, source))
    return out_band, out_doc


def plain_program(
    q_band, k_band, v_band, sink_band, q_doc, k_doc, v_doc, sink_doc, doc_starts, source_lists
):
    rows = q_band.shape[0]
    heads = k_band.shape[1] // HD
    shard = lax.axis_index("seq")

    def place(*dists):
        return jnp.stack([shard, 0, 0, 0, *dists]).astype(jnp.int32)

    rim = jnp.concatenate([k_band[rows - WIN :], v_band[rows - WIN :]], axis=1)
    rim = shifted(rim, 1)
    unit = jnp.concatenate([k_doc, v_doc], axis=1)
    units = [unit] + [shifted(unit, d) for d in range(1, BACK + 1)]
    band = band_call(
        place(), doc_starts, sink_band, q_band, k_band, v_band, rim, heads, rows, False, None
    )[0]
    plan = DocPlan(True, True, 1, heads, 0, BACK + 1, rows, False)
    doc = doc_call(
        plan, place(*range(BACK + 1)), doc_starts, sink_doc, (source_lists,),
        (q_doc,), units, None, None,
    )[0]
    return relay(band), relay(doc)


def solution(mesh):
    placed = (
        P("seq", "kv"),
        P("seq", "kv"),
        P("seq", "kv"),
        P("kv"),
        P("seq", "kv"),
        P("seq", "kv"),
        P("seq", "kv"),
        P("kv"),
        P(),
        P("seq", None),
    )

    def per_device(*args):
        heads = args[1].shape[1] // HD
        even = heads % 4 == 0 and mesh.shape["kv"] == 2 and mesh.shape["seq"] % 4 == 0
        return (paired_program if even else plain_program)(*args)

    return jax.shard_map(
        per_device,
        mesh=mesh,
        in_specs=placed,
        out_specs=(P(("seq", "kv"), None), P(("seq", "kv"), None)),
        check_vma=False,
    )
```
